32 devices in a mesh: rows: 8 (over z, y), cols: 4 (over x, core).
Axes of the slice: x: 2, y: 2, z: 4, core: 2. Of those that a mesh axis runs over, the one named last changes fastest.
Arguments:
- snapshot: float32 [3072, 8192], P('rows', 'cols'), may hold values from -270 to 270
- test_matrix: float32 [8192, 256], P('cols'), may hold values from -0.0625 to 0.0625
Outputs:
- projected: float32 [8192, 256], P('cols')
- triangle: float32 [256, 256], replicated
The draws below stay inside these ranges and needn't reach their ends.
All inputs are finite; a program needn't handle non-finite values.
Results may differ from the reference program's by a relative error of at most 0.00007.
Values sent between devices are 32-bit elements; how exact they have to be, the bound alone decides.
No kernel may reach another device: no remote copies, remote signals or barrier semaphores. Data moves between devices by JAX's collectives and lax.ppermute only.
A program may use at most 64 MiB of HBM per device.

```python
import math
import jax
import jax.numpy as jnp
from jax import lax

SNAPSHOTS = 8192
SKETCH = 256
POINTS_DEV = 384
POINTS = 3072
N_ROWS = 8


def draw_snapshot(key, part):
    base_key = jax.random.fold_in(key, 11)
    key_rows, key_cols, key_main = jax.random.split(base_key, 3)
    total = POINTS_DEV * N_ROWS
    rise_rows = 1.0 + 2.0 * jnp.arange(total, dtype=jnp.float32) / (total - 1)
    row_scale = rise_rows * jnp.exp(jax.random.uniform(key_rows, (total,), jnp.float32, 0.0, math.log(10.0)))
    rise_cols = 1.0 + 2.0 * jnp.arange(SNAPSHOTS, dtype=jnp.float32) / (SNAPSHOTS - 1)
    col_scale = rise_cols * jnp.exp(jax.random.uniform(key_cols, (SNAPSHOTS,), jnp.float32, 0.0, math.log(2.0)))
    values = jnp.clip(jax.random.normal(key_main, (total, SNAPSHOTS), jnp.float32), -6.0, 6.0)
    return (values * row_scale[:, None] * col_scale[None, :] * 0.25).astype(jnp.float32)


def level_of(own_key, extent, cuts, smallest, top_value):
    loudness, own = 1.0, jax.random.fold_in(own_key, 6)
    for position, blocks in cuts:
        heights = jnp.exp(jax.random.uniform(jax.random.fold_in(own, position), (blocks,), jnp.float32, smallest / len(cuts), top_value / len(cuts)))
        loudness = loudness * jnp.repeat(heights, extent[position] // blocks).reshape([-1 if axis == position else 1 for axis in range(len(extent))])
    return loudness


def bell_draw(key, dims, scale, reach, pieces=(), kind=jnp.bfloat16):
    array = jax.random.normal(key, dims, jnp.float32) * scale
    if len(pieces) > 0:
        array = level_of(key, dims, pieces, -0.22, 0.18) * array
    return jnp.clip(array, min=-reach, max=reach).astype(kind)


def setup_inputs(seed: int = 0) -> dict:
    key_of = jax.random.split(jax.random.key(seed), 3)
    return {
        "snapshot": draw_snapshot(jax.random.fold_in(key_of[2], 71), 0),
        "test_matrix": bell_draw(key_of[1], (SNAPSHOTS, SKETCH), SNAPSHOTS ** -0.5, 0.0625, ((0, 4),), jnp.float32),
    }


def reference(snapshot, test_matrix):
    high = lax.Precision.HIGHEST
    sketch = jnp.dot(snapshot.astype(jnp.float32), test_matrix.astype(jnp.float32), precision=high, preferred_element_type=jnp.float32)
    gram = jnp.dot(sketch.T.astype(jnp.float32), sketch.astype(jnp.float32), precision=high, preferred_element_type=jnp.float32)
    lower = jnp.linalg.cholesky(gram)
    basis_t = jax.scipy.linalg.solve_triangular(lower, sketch.T, lower=True)
    projected = jnp.dot(snapshot.T.astype(jnp.float32), basis_t.T.astype(jnp.float32), precision=high, preferred_element_type=jnp.float32)
    triangle = lower.T / jnp.sqrt(jnp.float32(POINTS))
    return (projected, triangle)
```

```python
import functools

import jax
import jax.numpy as jnp
from jax import lax
from jax.experimental import pallas as pl
from jax.experimental.pallas import tpu as pltpu
from jax.sharding import PartitionSpec as P

high = lax.Precision.HIGHEST


def mm(left, right, dims, precision=high):
    return lax.dot_general(
        left, right, (dims, ((), ())), precision=precision, preferred_element_type=jnp.float32
    )


def factor_kernel(block, panel, gram_ref, upper_ref, inverse_ref, both, part):
    n = gram_ref.shape[0]
    row = lax.broadcasted_iota(jnp.int32, (panel, n), 0)
    col = lax.broadcasted_iota(jnp.int32, (panel, n), 1)
    sub = lax.broadcasted_iota(jnp.int32, (block, 2 * n), 0)
    lanes = min(n, 128)

    def wide(v):
        return jnp.concatenate([v] * (2 * n // lanes), axis=1)

    for top in range(0, n, panel):
        eye = jnp.where(row + top == col, 1.0, 0.0).astype(jnp.float32)
        rest = jnp.concatenate([gram_ref[top : top + panel, :], eye], axis=1)
        if top:
            rest = rest - mm(both[:top, top : top + panel], both[:top, :], ((0,), (0,)))
        part[...] = rest
        for inner in range(0, panel, block):
            k = top + inner
            rows = part[inner : inner + block, :]
            columns = [
                jnp.broadcast_to(rows[:, k + j : k + j + 1], (block, lanes)) for j in range(block)
            ]
            d = {
                (i, j): jnp.broadcast_to(columns[j][i : i + 1, :], (block, lanes))
                for i in range(block)
                for j in range(i, block)
            }
            scale = []
            for i in range(block):
                scale.append(lax.rsqrt(d[i, i]))
                for j in range(i + 1, block):
                    d[i, j] = d[i, j] * scale[i]
                for j in range(i + 1, block):
                    for l in range(j, block):
                        d[j, l] = d[j, l] - d[i, j] * d[i, l]
            done, solved = [], jnp.zeros((block, 2 * n), jnp.float32)
            for i in range(block):
                line = jnp.broadcast_to(rows[i : i + 1, :], (block, 2 * n))
                for m in range(i):
                    line = line - wide(d[m, i]) * done[m]
                line = line * wide(scale[i])
                done.append(line)
                solved = jnp.where(sub == i, line, solved)
            both[k : k + block, :] = solved
            if inner + block < panel:
                part[inner + block :, :] -= mm(
                    solved[:, k + block : top + panel], solved, ((0,), (0,))
                )
    across = lax.broadcasted_iota(jnp.int32, (n, n), 1)
    down = lax.broadcasted_iota(jnp.int32, (n, n), 0)
    upper_ref[...] = jnp.where(down <= across, both[:, :n], 0.0)
    inverse_ref[...] = both[:, n:]


def factor(gram):
    n = gram.shape[0]
    panel = min(n, 64)
    whole = pl.BlockSpec(memory_space=pltpu.VMEM)
    return pl.pallas_call(
        functools.partial(factor_kernel, 8, panel),
        out_shape=(jax.ShapeDtypeStruct((n, n), jnp.float32),) * 2,
        in_specs=[whole],
        out_specs=(whole, whole),
        scratch_shapes=[
            pltpu.VMEM((n, 2 * n), jnp.float32),
            pltpu.VMEM((panel, 2 * n), jnp.float32),
        ],
        cost_estimate=pl.CostEstimate(
            flops=12 * n**3, bytes_accessed=12 * n * n, transcendentals=n
        ),
        name="factor",
    )(gram)


def swap(value, axis, mask):
    return lax.ppermute(value, axis, [(i, i ^ mask) for i in range(lax.axis_size(axis))])


def rows_of(value, start, size):
    return lax.dynamic_slice_in_dim(value, start, size, 0)


def join(bit, mine, other):
    size = mine.shape[0]
    out = jnp.zeros((2 * size,) + mine.shape[1:], mine.dtype)
    out = lax.dynamic_update_slice_in_dim(out, mine, bit * size, 0)
    return lax.dynamic_update_slice_in_dim(out, other, (1 - bit) * size, 0)


def sum_over_columns(value, axis):
    n = lax.axis_size(axis)
    if n == 1:
        return value
    bit = lax.axis_index(axis) & 1
    half = value.shape[0] // 2
    mine = rows_of(value, bit * half, half) + swap(rows_of(value, (1 - bit) * half, half), axis, 1)
    mask = 2
    while mask < n:
        mine = mine + swap(mine, axis, mask)
        mask *= 2
    return join(bit, mine, swap(mine, axis, 1))


def sum_by_doubling(value, axis):
    n = lax.axis_size(axis)
    step, mask = 1, 1
    while step < n:
        value = value + swap(value, axis, mask)
        step *= 2
        mask = 2 * step - 2 if step > 1 else 1
    return value


class Ring:
    def __init__(self, axis):
        self.axis = axis
        total = lax.axis_size(axis)
        self.length = total // 2
        index = lax.axis_index(axis)
        self.side = index & 1
        self.place = index >> 1

    def send(self, value, way):
        n = 2 * self.length
        return lax.ppermute(value, self.axis, [(i, (i + 2 * way) % n) for i in range(n)])

    def slab(self, value, away):
        size = value.shape[0] // self.length
        at = lax.rem(self.place + away + 2 * self.length, self.length)
        return rows_of(value, at * size, size)

    def halve(self, value):
        half = value.shape[0] // 2
        mine = rows_of(value, self.side * half, half)
        return mine, swap(rows_of(value, (1 - self.side) * half, half), self.axis, 1)

    def scatter_steps(self, value):
        far = self.length // 2
        size = value.shape[0] // self.length
        half = size // 2
        right = left = None
        for step in range(far):
            ahead = self.slab(value, far - step)
            behind = self.slab(value, step - far)
            if step == 0:
                right, left = ahead[:half], behind[half:]
            else:
                if step == 1:
                    right = jnp.concatenate([ahead[:half] + right, ahead[half:]])
                    left = jnp.concatenate([behind[:half], behind[half:] + left])
                else:
                    right, left = ahead + right, behind + left
            right, left = self.send(right, 1), self.send(left, -1)
            yield
        own = self.slab(value, 0)
        if far == 1:
            self.result = own + jnp.concatenate([right, left])
        else:
            self.result = own + (right + left)

    def gather_steps(self, own):
        far = self.length // 2
        size = own.shape[0]
        half = size // 2
        out = jnp.zeros((size * self.length,) + own.shape[1:], own.dtype)

        def put(out, value, away, offset=0):
            at = lax.rem(self.place + away + 2 * self.length, self.length)
            return lax.dynamic_update_slice_in_dim(out, value, at * size + offset, 0)

        out = put(out, own, 0)
        right = left = own
        for step in range(1, far + 1):
            if step == far:
                right, left = right[:half], left[half:]
            right, left = self.send(right, 1), self.send(left, -1)
            yield
            out = put(out, right, -step)
            out = put(out, left, step, half if step == far else 0)
        self.result = out


def run(ring_axis, *makers):
    rings = [Ring(ring_axis) for _ in makers]
    live = [maker(ring) for maker, ring in zip(makers, rings)]
    for steps in live:
        for _ in steps:
            pass
    return [ring.result for ring in rings]


def sum_over_rows(value, axis):
    total = value.shape[0]
    ring = Ring(axis)
    unit = 32 * ring.length
    second = max(1, round(total * 7 / 16 / unit)) * unit
    first = total - second
    one, two = value[:first], value[first:]
    mine, got = ring.halve(two)
    (one,) = run(axis, lambda r: r.scatter_steps(one))
    two = mine + got
    mine, got = ring.halve(one)
    (two,) = run(axis, lambda r: r.scatter_steps(two))
    one = mine + got
    got = swap(one, axis, 1)
    (two,) = run(axis, lambda r: r.gather_steps(two))
    one = join(ring.side, one, got)
    got = swap(two, axis, 1)
    (one,) = run(axis, lambda r: r.gather_steps(one))
    two = join(ring.side, two, got)
    return jnp.concatenate([one, two])


def body(snapshot, test_matrix):
    width = test_matrix.shape[1]
    sketch = sum_over_columns(mm(snapshot, test_matrix, ((1,), (0,))), "cols")
    columns = lax.axis_size("cols")
    part = width // 2
    bit = lax.axis_index("cols") & 1
    strip = lax.dynamic_slice_in_dim(sketch, bit * part, part, 1)
    strip = sum_by_doubling(mm(strip, sketch, ((0,), (0,))), "rows")
    gram = join(bit, strip, swap(strip, "cols", 1)) if columns > 1 else strip
    upper, inverse = factor(gram)
    product = sum_over_rows(mm(snapshot, sketch, ((0,), (0,))), "rows")
    projected = mm(product, inverse, ((1,), (1,)))
    total = snapshot.shape[0] * lax.axis_size("rows")
    return (projected, upper / jnp.sqrt(jnp.float32(total)))


def solution(mesh):
    return jax.shard_map(
        body,
        mesh=mesh,
        in_specs=(P("rows", "cols"), P("cols", None)),
        out_specs=(P("cols", None), P()),
        check_vma=False,
    )
```

```python
import functools

import jax
import jax.numpy as jnp
from jax import lax
from jax.experimental import pallas as pl
from jax.experimental.pallas import tpu as pltpu
from jax.sharding import PartitionSpec as P

high = lax.Precision.HIGHEST
VMEM = pl.BlockSpec(memory_space=pltpu.VMEM)
ANY = pl.BlockSpec(memory_space=pltpu.HBM)
F32, BF16 = jnp.float32, jnp.bfloat16
MIB = 1 << 20


def mm(left, right, dims, precision=high):
    return lax.dot_general(
        left, right, (dims, ((), ())), precision=precision, preferred_element_type=F32
    )


def split(value):
    top = value.astype(BF16)
    return top, (value - top.astype(F32)).astype(BF16)


def mm3(left, right, dims):
    def one(a, b):
        return lax.dot_general(a, b, (dims, ((), ())), preferred_element_type=F32)

    return one(left[0], right[0]) + (one(left[0], right[1]) + one(left[1], right[0]))


def array(shape, dtype=F32):
    return jax.ShapeDtypeStruct(shape, dtype)


def call(kernel, name, outs, *args, specs=None, out_specs=None, scratch=(), flops=0, vmem=8, **more):
    outs = tuple(outs)
    return pl.pallas_call(
        kernel,
        out_shape=outs,
        in_specs=specs or [VMEM] * len(args),
        out_specs=out_specs or (VMEM,) * len(outs),
        scratch_shapes=list(scratch),
        compiler_params=pltpu.CompilerParams(vmem_limit_bytes=vmem * MIB),
        cost_estimate=pl.CostEstimate(
            flops=flops,
            bytes_accessed=sum(a.size * a.dtype.itemsize for a in args),
            transcendentals=0,
        ),
        name=name,
        **more,
    )(*args)


def factor_kernel(block, panel, gram_ref, upper_ref, inverse_ref, both, part):
    n = gram_ref.shape[0]
    row = lax.broadcasted_iota(jnp.int32, (panel, n), 0)
    col = lax.broadcasted_iota(jnp.int32, (panel, n), 1)
    sub = lax.broadcasted_iota(jnp.int32, (block, 2 * n), 0)
    lanes = min(n, 128)

    def wide(v):
        return jnp.concatenate([v] * (2 * n // lanes), axis=1)

    for top in range(0, n, panel):
        eye = jnp.where(row + top == col, 1.0, 0.0).astype(jnp.float32)
        rest = jnp.concatenate([gram_ref[top : top + panel, :], eye], axis=1)
        if top:
            rest = rest - mm(both[:top, top : top + panel], both[:top, :], ((0,), (0,)))
        part[...] = rest
        for inner in range(0, panel, block):
            k = top + inner
            rows = part[inner : inner + block, :]
            columns = [
                jnp.broadcast_to(rows[:, k + j : k + j + 1], (block, lanes)) for j in range(block)
            ]
            d = {
                (i, j): jnp.broadcast_to(columns[j][i : i + 1, :], (block, lanes))
                for i in range(block)
                for j in range(i, block)
            }
            scale = []
            for i in range(block):
                scale.append(lax.rsqrt(d[i, i]))
                for j in range(i + 1, block):
                    d[i, j] = d[i, j] * scale[i]
                for j in range(i + 1, block):
                    for l in range(j, block):
                        d[j, l] = d[j, l] - d[i, j] * d[i, l]
            done, solved = [], jnp.zeros((block, 2 * n), jnp.float32)
            for i in range(block):
                line = jnp.broadcast_to(rows[i : i + 1, :], (block, 2 * n))
                for m in range(i):
                    line = line - wide(d[m, i]) * done[m]
                line = line * wide(scale[i])
                done.append(line)
                solved = jnp.where(sub == i, line, solved)
            both[k : k + block, :] = solved
            if inner + block < panel:
                part[inner + block :, :] -= mm(
                    solved[:, k + block : top + panel], solved, ((0,), (0,))
                )
    across = lax.broadcasted_iota(jnp.int32, (n, n), 1)
    down = lax.broadcasted_iota(jnp.int32, (n, n), 0)
    upper_ref[...] = jnp.where(down <= across, both[:, :n], 0.0)
    inverse_ref[...] = both[:, n:]


def factor(gram):
    n = gram.shape[0]
    panel = min(n, 64)
    return call(
        functools.partial(factor_kernel, 8, panel),
        "factor",
        (array((n, n)),) * 2,
        gram,
        scratch=[pltpu.VMEM((n, 2 * n), F32), pltpu.VMEM((panel, 2 * n), F32)],
        flops=12 * n**3,
    )


def sketch_kernel(axis, snap_any, test_any, mine_ref, other_ref, top_ref, rest_ref, snap, test, sems):
    depth = snap.shape[1]
    chunks = sems.shape[1]
    size = depth // chunks
    copies = []
    for c in range(chunks):
        part = pl.ds(c * size, size)
        copies.append(
            (
                pltpu.make_async_copy(snap_any.at[:, part], snap.at[:, part], sems.at[0, c]),
                pltpu.make_async_copy(test_any.at[part], test.at[part], sems.at[1, c]),
            )
        )
    for a, b in copies:
        b.start()
        a.start()
    total = None
    for c, (a, b) in enumerate(copies):
        b.wait()
        a.wait()
        part = slice(c * size, (c + 1) * size)
        left = split(snap[:, part])
        top_ref[:, part], rest_ref[:, part] = left
        term = mm3(left, split(test[part, :]), ((1,), (0,)))
        total = term if total is None else total + term
    half = total.shape[0] // 2
    first = lax.axis_index(axis) & 1
    low, high_ = total[:half], total[half:]
    mine_ref[...] = jnp.where(first == 0, low, high_)
    other_ref[...] = jnp.where(first == 0, high_, low)


def sketch_parts(snapshot, test_matrix, axis):
    points, depth = snapshot.shape
    width = test_matrix.shape[1]
    chunks = 4
    half = array((points // 2, width))
    return call(
        functools.partial(sketch_kernel, axis),
        "sketch",
        (half, half, array(snapshot.shape, BF16), array(snapshot.shape, BF16)),
        snapshot,
        test_matrix,
        specs=[ANY, ANY],
        scratch=[
            pltpu.VMEM(snapshot.shape, F32),
            pltpu.VMEM(test_matrix.shape, F32),
            pltpu.SemaphoreType.DMA((2, chunks)),
        ],
        flops=6 * points * depth * width,
        vmem=24,
    )


def swap(value, axis, mask):
    return lax.ppermute(value, axis, [(i, i ^ mask) for i in range(lax.axis_size(axis))])


def first_bit(axis):
    return lax.axis_index(axis) & 1


def ordered(axis, mine, other):
    low = first_bit(axis) == 0
    return jnp.where(low, mine, other), jnp.where(low, other, mine)


def strip_kernel(axis, mine_ref, other_ref, out_ref, scratch):
    half = mine_ref.shape[0]
    bit = first_bit(axis)
    scratch[pl.ds(pl.multiple_of(bit * half, half), half), :] = mine_ref[...]
    scratch[pl.ds(pl.multiple_of((1 - bit) * half, half), half), :] = other_ref[...]
    width = out_ref.shape[0]
    left = scratch[:, pl.ds(pl.multiple_of(bit * width, width), width)]
    out_ref[...] = mm(left, scratch[...], ((0,), (0,)))


def gram_strip(mine, other, axis):
    half, width = mine.shape
    (out,) = call(
        functools.partial(strip_kernel, axis),
        "strip",
        [array((width // 2, width))],
        mine,
        other,
        scratch=[pltpu.VMEM((2 * half, width), F32)],
        flops=6 * half * width * width,
    )
    return out


class Slabs:
    def __init__(self, axis):
        self.axis = axis
        self.total = lax.axis_size(axis)
        self.length = self.total // 2

    def owner(self, places, across):
        index = lax.axis_index(self.axis)
        place = lax.rem((index >> 1) + (places % self.length), self.length)
        return place * 2 + ((index & 1) ^ across)

    def send(self, value, places, across):
        pairs = [
            (i, ((i >> 1) + places) % self.length * 2 + ((i & 1) ^ across)) for i in range(self.total)
        ]
        return lax.ppermute(value, self.axis, pairs)


def product_kernel(slabs, axis, groups, first, *refs):
    if first:
        mine_ref, other_ref, top_ref, rest_ref, stop_ref, srest_ref, *outs = refs
        half = mine_ref.shape[0]
        bit = first_bit(axis)
        for ref, at in ((mine_ref, bit), (other_ref, 1 - bit)):
            where = pl.ds(pl.multiple_of(at * half, half), half)
            stop_ref[where, :], srest_ref[where, :] = split(ref[...])
    else:
        stop_ref, srest_ref, top_ref, rest_ref, *outs = refs
    right = (stop_ref[...], srest_ref[...])
    for group, out in zip(groups, outs):
        size = out.shape[0] // len(group)
        for n, (places, across) in enumerate(group):
            at = pl.ds(pl.multiple_of(slabs.owner(places, across) * size, size), size)
            left = (top_ref[:, at], rest_ref[:, at])
            out[n * size : (n + 1) * size, :] = mm3(left, right, ((0,), (0,)))


def products(slabs, axis, groups, first, one, two, top, rest):
    points, columns = top.shape
    width = one.shape[1]
    size = columns // slabs.total
    outs = [array((size * len(group), width)) for group in groups]
    if first:
        outs = [array((points, width), BF16)] * 2 + outs
    return call(
        functools.partial(product_kernel, slabs, axis, groups, first),
        "product",
        outs,
        one,
        two,
        top,
        rest,
        flops=6 * points * width * size * sum(map(len, groups)),
        vmem=12,
    )


def final_kernel(slabs, groups, inverse_ref, *refs):
    count = len(groups)
    pieces, refs = refs[:count], refs[count:]
    out_any, held, sems = refs[-3:]
    right = split(inverse_ref[...])
    copies = []
    n = 0
    for group, piece in zip(groups, pieces):
        size = piece.shape[0] // len(group)
        for g, (places, across) in enumerate(group):
            held[n] = mm3(split(piece[g * size : (g + 1) * size, :]), right, ((1,), (1,)))
            at = pl.ds(pl.multiple_of(slabs.owner(places, across) * size, size), size)
            copy = pltpu.make_async_copy(held.at[n], out_any.at[at], sems.at[n])
            copy.start()
            copies.append(copy)
            n += 1
    for copy in copies:
        copy.wait()


def final(slabs, groups, inverse, pieces, before=None):
    width = inverse.shape[0]
    count = sum(map(len, groups))
    size = pieces[0].shape[0] // len(groups[0])
    args = [inverse, *pieces]
    specs = [VMEM] * len(args)
    more = {}
    if before is not None:
        more["input_output_aliases"] = {len(args): 0}
        args.append(before)
        specs.append(ANY)
    (out,) = call(
        functools.partial(final_kernel, slabs, groups),
        "final",
        [array((size * slabs.total, width))],
        *args,
        specs=specs,
        out_specs=(ANY,),
        scratch=[pltpu.VMEM((count, size, width), F32), pltpu.SemaphoreType.DMA((count,))],
        flops=6 * count * size * width * width,
        **more,
    )
    return out


def body(snapshot, test_matrix):
    mine, other, top, rest = sketch_parts(snapshot, test_matrix, "cols")
    columns = lax.axis_size("cols")
    mine = mine + swap(other, "cols", 1)
    mask = 2
    while mask < columns:
        mine = mine + swap(mine, "cols", mask)
        mask *= 2
    other = swap(mine, "cols", 1)

    slabs = Slabs("rows")
    assert slabs.length == 4
    stop, srest, far, pair, back = products(
        slabs, "cols", [[(2, 1)], [(1, 1)], [(-1, 1), (-2, 0)]], True, mine, other, top, rest
    )
    far = slabs.send(far, 2, 1)
    back = slabs.send(back, -1, 0)
    pair = slabs.send(pair, 0, 1)
    strip = gram_strip(mine, other, "cols")
    own, across, ahead, behind = products(
        slabs, "cols", [[(0, 0)], [(0, 1)], [(1, 0)], [(-1, 0)]], False, stop, srest, top, rest
    )
    step, mask = 1, 1
    while step < slabs.total:
        strip = strip + swap(strip, "rows", mask)
        step *= 2
        mask = 2 * step - 2
    gram = jnp.concatenate(ordered("cols", strip, swap(strip, "cols", 1)))
    upper, inverse = factor(gram)
    size = own.shape[0]
    across = slabs.send(across + back[:size], 0, 1)
    behind = slabs.send(behind + back[size:], -1, 0)
    ahead = slabs.send(ahead + pair, 1, 0)
    own = (own + far) + (across + behind + ahead)
    far = slabs.send(own, -2, 1)
    across = slabs.send(own, 0, 1)
    behind = slabs.send(own, 1, 0)
    ahead = slabs.send(own, -1, 0)
    pair = slabs.send(ahead, 0, 1)
    back = slabs.send(jnp.concatenate([across, behind]), 1, 0)
    out = final(
        slabs, [[(0, 0)], [(0, 1)], [(1, 0)], [(-1, 0)]], inverse, [own, across, ahead, behind]
    )
    projected = final(
        slabs, [[(1, 1)], [(-1, 1), (-2, 0)], [(2, 1)]], inverse, [pair, back, far], out
    )
    total = snapshot.shape[0] * lax.axis_size("rows")
    return (projected, upper / jnp.sqrt(jnp.float32(total)))


def plain_body(snapshot, test_matrix):
    sketch = lax.psum(mm(snapshot, test_matrix, ((1,), (0,))), "cols")
    gram = lax.psum(mm(sketch, sketch, ((0,), (0,))), "rows")
    upper, inverse = factor(gram)
    product = lax.psum(mm(snapshot, sketch, ((0,), (0,))), "rows")
    total = snapshot.shape[0] * lax.axis_size("rows")
    return (mm(product, inverse, ((1,), (1,))), upper / jnp.sqrt(jnp.float32(total)))


def solution(mesh):
    return jax.shard_map(
        body if mesh.shape["rows"] == 8 else plain_body,
        mesh=mesh,
        in_specs=(P("rows", "cols"), P("cols", None)),
        out_specs=(P("cols", None), P()),
        check_vma=False,
    )
```

```python
import functools

import jax
import jax.numpy as jnp
from jax import lax
from jax.experimental import pallas as pl
from jax.experimental.pallas import tpu as pltpu
from jax.sharding import PartitionSpec as P


high = lax.Precision.HIGHEST
VMEM = pl.BlockSpec(memory_space=pltpu.VMEM)
ANY = pl.BlockSpec(memory_space=pltpu.HBM)
F32, BF16 = jnp.float32, jnp.bfloat16
MIB = 1 << 20


def mm(left, right, dims, precision=high):
    return lax.dot_general(
        left, right, (dims, ((), ())), precision=precision, preferred_element_type=F32
    )


def split(value):
    top = value.astype(BF16)
    return top, (value - top.astype(F32)).astype(BF16)


def mm3(left, right, dims):
    def one(a, b):
        return lax.dot_general(a, b, (dims, ((), ())), preferred_element_type=F32)

    return one(left[0], right[0]) + (one(left[0], right[1]) + one(left[1], right[0]))


def array(shape, dtype=F32):
    return jax.ShapeDtypeStruct(shape, dtype)


def call(kernel, outs, *args, specs=None, out_specs=None, scratch=(), flops=0, vmem=8, **more):
    outs = tuple(outs)
    return pl.pallas_call(
        kernel,
        out_shape=outs,
        in_specs=specs or [VMEM] * len(args),
        out_specs=out_specs or (VMEM,) * len(outs),
        scratch_shapes=list(scratch),
        compiler_params=pltpu.CompilerParams(vmem_limit_bytes=vmem * MIB),
        cost_estimate=pl.CostEstimate(
            flops=flops,
            bytes_accessed=sum(a.size * a.dtype.itemsize for a in args),
            transcendentals=0,
        ),
        **more,
    )(*args)


def factor_kernel(block, top, gram_ref, *refs):
    *above, out_ref, part = refs
    panel, n = out_ref.shape[0], gram_ref.shape[0]
    row = lax.broadcasted_iota(jnp.int32, (panel, n), 0)
    col = lax.broadcasted_iota(jnp.int32, (panel, n), 1)
    sub = lax.broadcasted_iota(jnp.int32, (block, 2 * n), 0)
    lanes = min(n, 128)

    def wide(v):
        return jnp.concatenate([v] * (2 * n // lanes), axis=1)

    eye = jnp.where(row + top == col, 1.0, 0.0).astype(F32)
    rest = jnp.concatenate([gram_ref[top : top + panel, :], eye], axis=1)
    for ref in above:
        rest = rest - mm(ref[:, top : top + panel], ref[...], ((0,), (0,)))
    part[...] = rest
    for inner in range(0, panel, block):
        k = top + inner
        rows = part[inner : inner + block, :]
        columns = [
            jnp.broadcast_to(rows[:, k + j : k + j + 1], (block, lanes)) for j in range(block)
        ]
        d = {
            (i, j): jnp.broadcast_to(columns[j][i : i + 1, :], (block, lanes))
            for i in range(block)
            for j in range(i, block)
        }
        scale = []
        for i in range(block):
            scale.append(lax.rsqrt(d[i, i]))
            for j in range(i + 1, block):
                d[i, j] = d[i, j] * scale[i]
            for j in range(i + 1, block):
                for l in range(j, block):
                    d[j, l] = d[j, l] - d[i, j] * d[i, l]
        done, solved = [], jnp.zeros((block, 2 * n), F32)
        for i in range(block):
            line = jnp.broadcast_to(rows[i : i + 1, :], (block, 2 * n))
            for m in range(i):
                line = line - wide(d[m, i]) * done[m]
            line = line * wide(scale[i])
            done.append(line)
            solved = jnp.where(sub == i, line, solved)
        out_ref[inner : inner + block, :] = solved
        if inner + block < panel:
            part[inner + block :, :] -= mm(
                solved[:, k + block : top + panel], solved, ((0,), (0,))
            )


def factor_rows(gram, above):
    n = gram.shape[0]
    panel = min(n, 64)
    top = panel * len(above)
    (rows,) = call(
        functools.partial(factor_kernel, 8, top),
        [array((panel, 2 * n))],
        gram,
        *above,
        scratch=[pltpu.VMEM((panel, 2 * n), F32)],
        flops=12 * n**3 // 4,
    )
    return rows


def upper_part(panels):
    n = panels[0].shape[1] // 2
    whole = jnp.concatenate([p[:, :n] for p in panels])
    return jnp.triu(whole)


def lower_part(panels):
    n = panels[0].shape[1] // 2
    return jnp.concatenate([p[:, n:] for p in panels])


def sketch_kernel(axis, snap_any, test_any, mine_ref, other_ref, top_ref, rest_ref, snap, test, sems):
    depth = snap.shape[1]
    chunks = sems.shape[1]
    size = depth // chunks
    copies = []
    for c in range(chunks):
        part = pl.ds(c * size, size)
        copies.append(
            (
                pltpu.make_async_copy(snap_any.at[:, part], snap.at[:, part], sems.at[0, c]),
                pltpu.make_async_copy(test_any.at[part], test.at[part], sems.at[1, c]),
            )
        )
    for a, b in copies:
        b.start()
        a.start()
    total = None
    for c, (a, b) in enumerate(copies):
        b.wait()
        a.wait()
        part = slice(c * size, (c + 1) * size)
        left = split(snap[:, part])
        top_ref[:, part], rest_ref[:, part] = left
        term = mm3(left, split(test[part, :]), ((1,), (0,)))
        total = term if total is None else total + term
    half = total.shape[0] // 2
    first = lax.axis_index(axis) & 1
    low, high_ = total[:half], total[half:]
    mine_ref[...] = jnp.where(first == 0, low, high_)
    other_ref[...] = jnp.where(first == 0, high_, low)


def sketch_parts(snapshot, test_matrix, axis):
    points, depth = snapshot.shape
    width = test_matrix.shape[1]
    chunks = 4
    half = array((points // 2, width))
    return call(
        functools.partial(sketch_kernel, axis),
        (half, half, array(snapshot.shape, BF16), array(snapshot.shape, BF16)),
        pltpu.with_memory_space_constraint(snapshot, pltpu.HBM),
        pltpu.with_memory_space_constraint(test_matrix, pltpu.HBM),
        specs=[ANY, ANY],
        scratch=[
            pltpu.VMEM(snapshot.shape, F32),
            pltpu.VMEM(test_matrix.shape, F32),
            pltpu.SemaphoreType.DMA((2, chunks)),
        ],
        flops=6 * points * depth * width,
        vmem=24,
    )


def swap(value, axis, mask):
    return lax.ppermute(value, axis, [(i, i ^ mask) for i in range(lax.axis_size(axis))])


def first_bit(axis):
    return lax.axis_index(axis) & 1


def ordered(axis, mine, other):
    low = first_bit(axis) == 0
    return jnp.where(low, mine, other), jnp.where(low, other, mine)


def strip_kernel(axis, mine_ref, other_ref, out_ref, scratch):
    half = mine_ref.shape[0]
    bit = first_bit(axis)
    scratch[pl.ds(pl.multiple_of(bit * half, half), half), :] = mine_ref[...]
    scratch[pl.ds(pl.multiple_of((1 - bit) * half, half), half), :] = other_ref[...]
    width = out_ref.shape[1]
    left = scratch[:, pl.ds(pl.multiple_of(bit * width, width), width)]
    out_ref[:width, :] = mm(left, left, ((0,), (0,)))
    cross = mm(scratch[:, :width], scratch[:, width:], ((0,), (0,)))
    out_ref[width:, :] = jnp.where(bit == 0, cross[: width // 2], cross[width // 2 :])


def gram_part(mine, other, axis):
    half, width = mine.shape
    block = width // 2
    (out,) = call(
        functools.partial(strip_kernel, axis),
        [array((block + block // 2, block))],
        mine,
        other,
        scratch=[pltpu.VMEM((2 * half, width), F32)],
        flops=6 * half * width * width,
    )
    return out


def gram_upper(axis, mine, other):
    first, second = ordered(axis, mine, other)
    block = first.shape[1]
    cross = jnp.concatenate([first[block:], second[block:]])
    above = jnp.concatenate([first[:block], cross], axis=1)
    below = jnp.concatenate([jnp.zeros_like(cross), second[:block]], axis=1)
    return jnp.concatenate([above, below])


class Ring:
    def __init__(self, axis):
        self.axis = axis
        self.length = lax.axis_size(axis)

    def slab(self, ahead):
        index = lax.axis_index(self.axis)
        place = index >> 1
        here = jnp.where((index & 1) == 0, place, self.length - 1 - place)
        return lax.rem(here + (ahead % self.length), self.length)

    def row(self, position):
        n = self.length
        position %= n
        return 2 * position if 2 * position < n else 2 * (n - 1 - position) + 1

    def send(self, value, way):
        pairs = [(self.row(p), self.row(p + way)) for p in range(self.length)]
        return lax.ppermute(value, self.axis, pairs)


def product_kernel(ring, axis, aheads, first, *refs):
    if first:
        mine_ref, other_ref, top_ref, rest_ref, stop_ref, srest_ref, *outs = refs
        half = mine_ref.shape[0]
        bit = first_bit(axis)
        for ref, at in ((mine_ref, bit), (other_ref, 1 - bit)):
            where = pl.ds(pl.multiple_of(at * half, half), half)
            stop_ref[where, :], srest_ref[where, :] = split(ref[...])
    else:
        stop_ref, srest_ref, top_ref, rest_ref, *outs = refs
    right = (stop_ref[...], srest_ref[...])
    for ahead, out in zip(aheads, outs):
        size = out.shape[0]
        at = pl.ds(pl.multiple_of(ring.slab(ahead) * size, size), size)
        out[...] = mm3((top_ref[:, at], rest_ref[:, at]), right, ((0,), (0,)))


def products(ring, axis, aheads, first, one, two, top, rest):
    points, columns = top.shape
    width = one.shape[1]
    size = columns // ring.length
    outs = [array((size, width))] * len(aheads)
    if first:
        outs = [array((points, width), BF16)] * 2 + outs
    return call(
        functools.partial(product_kernel, ring, axis, aheads, first),
        outs,
        one,
        two,
        top,
        rest,
        flops=6 * points * width * size * len(aheads),
        vmem=12,
    )


def final_kernel(ring, places, panels, *refs):
    count = len(places)
    lower = refs[:panels]
    pieces, refs = refs[panels : panels + count], refs[panels + count :]
    out_any, held, sems = refs[-3:]
    n = held.shape[2]
    size = out_any.shape[0] // ring.length
    right = split(jnp.concatenate([ref[:, n:] for ref in lower]))
    copies = []
    for i, ((ahead, offset), piece) in enumerate(zip(places, pieces)):
        rows = piece.shape[0]
        held[i, :rows] = mm3(split(piece[...]), right, ((1,), (1,)))
        at = pl.ds(pl.multiple_of(ring.slab(ahead) * size + offset, rows), rows)
        copy = pltpu.make_async_copy(held.at[i, pl.ds(0, rows)], out_any.at[at], sems.at[i])
        copy.start()
        copies.append(copy)
    for copy in copies:
        copy.wait()


def final(ring, pieces, panels, size, before=None):
    width = panels[0].shape[1] // 2
    args = [*panels, *pieces.values()]
    specs = [VMEM] * len(args)
    more = {}
    if before is not None:
        more["input_output_aliases"] = {len(args): 0}
        args.append(before)
        specs.append(ANY)
    count = len(pieces)
    (out,) = call(
        functools.partial(final_kernel, ring, tuple(pieces), len(panels)),
        [array((size * ring.length, width))],
        *args,
        specs=specs,
        out_specs=(ANY,),
        scratch=[pltpu.VMEM((count, size, width), F32), pltpu.SemaphoreType.DMA((count,))],
        flops=6 * sum(p.shape[0] for p in pieces.values()) * width * width,
        **more,
    )
    return out


def body(snapshot, test_matrix):
    return steps(snapshot, test_matrix)


def steps(snapshot, test_matrix):
    mine, other, top, rest = sketch_parts(snapshot, test_matrix, "cols")
    columns = lax.axis_size("cols")
    mine = mine + swap(other, "cols", 1)
    mask = 2
    while mask < columns:
        mine = mine + swap(mine, "cols", mask)
        mask *= 2
    other = swap(mine, "cols", 1)

    ring = Ring("rows")
    far = ring.length // 2
    stop, srest, part = products(ring, "cols", [far], True, mine, other, top, rest)
    size = part.shape[0]
    half = size // 2
    right, left = part[:half], part[half:]
    right = ring.send(right, 1)
    left = ring.send(left, -1)
    strip = gram_part(mine, other, "cols")
    step = 1
    while step < ring.length:
        strip = strip + swap(strip, "rows", step)
        step *= 2
    gram = gram_upper("cols", strip, swap(strip, "cols", 1))
    aheads = [sign * d for d in range(far - 1, 0, -1) for sign in (1, -1)] + [0]
    parts = products(ring, "cols", aheads, False, stop, srest, top, rest)
    parts = dict(zip(aheads, parts))
    for d in range(far - 1, 0, -1):
        if d == far - 1:
            right = jnp.pad(right, ((0, half), (0, 0)))
            left = jnp.pad(left, ((half, 0), (0, 0)))
        right = ring.send(parts[d] + right, 1)
        left = ring.send(parts[-d] + left, -1)
    own = parts[0] + (right + left)
    panels = []
    while len(panels) * 64 < gram.shape[0]:
        panels.append(factor_rows(gram, panels))
    early, late = {(0, 0): own}, {}
    right = left = own
    for d in range(1, far + 1):
        if d == far:
            right, left = right[:half], left[half:]
        right = ring.send(right, 1)
        left = ring.send(left, -1)
        held = early if d < far else late
        held[-d, 0] = right
        held[d, half if d == far else 0] = left
    out = final(ring, early, panels, size)
    projected = final(ring, late, panels, size, out)
    total = snapshot.shape[0] * lax.axis_size("rows")
    return (projected, upper_part(panels) / jnp.sqrt(jnp.float32(total)))


def plain_body(snapshot, test_matrix):
    sketch = lax.psum(mm(snapshot, test_matrix, ((1,), (0,))), "cols")
    gram = lax.psum(mm(sketch, sketch, ((0,), (0,))), "rows")
    panels = []
    while len(panels) * 64 < gram.shape[0]:
        panels.append(factor_rows(gram, panels))
    product = lax.psum(mm(snapshot, sketch, ((0,), (0,))), "rows")
    total = snapshot.shape[0] * lax.axis_size("rows")
    projected = mm(product, lower_part(panels), ((1,), (1,)))
    return (projected, upper_part(panels) / jnp.sqrt(jnp.float32(total)))


def solution(mesh):
    rows = mesh.shape["rows"]
    ring = rows == 8
    return jax.shard_map(
        body if ring else plain_body,
        mesh=mesh,
        in_specs=(P("rows", "cols"), P("cols", None)),
        out_specs=(P("cols", None), P()),
        check_vma=False,
    )
```

```python
import functools

import jax
import jax.numpy as jnp
from jax import lax
from jax.experimental import pallas as pl
from jax.experimental.pallas import tpu as pltpu
from jax.sharding import PartitionSpec as P


high = lax.Precision.HIGHEST
VMEM = pl.BlockSpec(memory_space=pltpu.VMEM)
ANY = pl.BlockSpec(memory_space=pltpu.HBM)
F32, BF16 = jnp.float32, jnp.bfloat16
MIB = 1 << 20
PANEL = 32


def mm(left, right, dims, precision=high):
    return lax.dot_general(
        left, right, (dims, ((), ())), precision=precision, preferred_element_type=F32
    )


def split(value):
    top = value.astype(BF16)
    return top, (value - top.astype(F32)).astype(BF16)


def mm3(left, right, dims):
    def one(a, b):
        return lax.dot_general(a, b, (dims, ((), ())), preferred_element_type=F32)

    return one(left[0], right[0]) + (one(left[0], right[1]) + one(left[1], right[0]))


def array(shape, dtype=F32):
    return jax.ShapeDtypeStruct(shape, dtype)


def call(kernel, outs, *args, specs=None, out_specs=None, scratch=(), flops=0, vmem=8, **more):
    outs = tuple(outs)
    return pl.pallas_call(
        kernel,
        out_shape=outs,
        in_specs=specs or [VMEM] * len(args),
        out_specs=out_specs or (VMEM,) * len(outs),
        scratch_shapes=list(scratch),
        compiler_params=pltpu.CompilerParams(vmem_limit_bytes=vmem * MIB),
        cost_estimate=pl.CostEstimate(
            flops=flops,
            bytes_accessed=sum(a.size * a.dtype.itemsize for a in args),
            transcendentals=0,
        ),
        **more,
    )(*args)


def factor_kernel(block, top, gram_ref, *refs):
    *above, out_ref, part = refs
    panel, n = out_ref.shape[0], gram_ref.shape[0]
    lanes, group = 128, 8
    row = lax.broadcasted_iota(jnp.int32, (panel, n), 0)
    col = lax.broadcasted_iota(jnp.int32, (panel, n), 1)
    low = top // lanes * lanes
    high_ = n + pl.cdiv(top + panel, lanes) * lanes
    width = high_ - low
    sub = lax.broadcasted_iota(jnp.int32, (group, width), 0)

    def wide(v):
        return jnp.concatenate([v] * (width // lanes), axis=1)

    eye = jnp.where(row + top == col, 1.0, 0.0).astype(F32)
    rest = jnp.concatenate([gram_ref[top : top + panel, :], eye], axis=1)[:, low:high_]
    for ref in above:
        rest = rest - mm(ref[:, top : top + panel], ref[:, low:high_], ((0,), (0,)))
    part[:, low:high_] = rest
    if low > 0:
        out_ref[:, :low] = jnp.zeros((panel, low), F32)
    if high_ < 2 * n:
        out_ref[:, high_:] = jnp.zeros((panel, 2 * n - high_), F32)
    for inner in range(0, panel, block):
        k = top + inner - low
        d, rows = {}, []
        for g in range(0, block, group):
            rows.append(part[inner + g : inner + g + group, low:high_])
            for j in range(g, block):
                c = jnp.broadcast_to(rows[-1][:, k + j : k + j + 1], (group, lanes))
                for i in range(g, min(g + group, j + 1)):
                    d[i, j] = jnp.broadcast_to(c[i - g : i - g + 1, :], (group, lanes))
        scale = []
        for i in range(block):
            scale.append(lax.rsqrt(d[i, i]))
            for j in range(i + 1, block):
                d[i, j] = d[i, j] * scale[i]
            for j in range(i + 1, block):
                for l in range(j, block):
                    d[j, l] = d[j, l] - d[i, j] * d[i, l]
        done, solved = [], []
        for i in range(block):
            g, at = divmod(i, group)
            if at == 0:
                solved.append(jnp.zeros((group, width), F32))
            line = jnp.broadcast_to(rows[g][at : at + 1, :], (group, width))
            for m in range(i):
                line = line - wide(d[m, i]) * done[m]
            line = line * wide(scale[i])
            done.append(line)
            solved[g] = jnp.where(sub == at, line, solved[g])
        solved = jnp.concatenate(solved)
        out_ref[inner : inner + block, low:high_] = solved
        if inner + block < panel:
            part[inner + block :, low:high_] -= mm(
                solved[:, k + block : top + panel - low], solved, ((0,), (0,))
            )


def factor_rows(gram, above):
    n = gram.shape[0]
    panel = min(n, PANEL)
    top = panel * len(above)
    (rows,) = call(
        functools.partial(factor_kernel, 16, top),
        [array((panel, 2 * n))],
        gram,
        *above,
        scratch=[pltpu.VMEM((panel, 2 * n), F32)],
        flops=12 * n * n * panel,
    )
    return rows


def upper_part(panels):
    n = panels[0].shape[1] // 2
    whole = jnp.concatenate([p[:, :n] for p in panels])
    return jnp.triu(whole)


def lower_part(panels):
    n = panels[0].shape[1] // 2
    return jnp.concatenate([p[:, n:] for p in panels])


def sketch_kernel(axis, snap_any, test_any, mine_ref, other_ref, top_ref, rest_ref, snap, test, sems):
    depth = snap.shape[1]
    chunks = sems.shape[1]
    size = depth // chunks
    copies = []
    for c in range(chunks):
        part = pl.ds(c * size, size)
        copies.append(
            (
                pltpu.make_async_copy(snap_any.at[:, part], snap.at[:, part], sems.at[0, c]),
                pltpu.make_async_copy(test_any.at[part], test.at[part], sems.at[1, c]),
            )
        )
    for a, b in copies:
        b.start()
        a.start()
    total = None
    for c, (a, b) in enumerate(copies):
        b.wait()
        a.wait()
        part = slice(c * size, (c + 1) * size)
        left = split(snap[:, part])
        top_ref[:, part], rest_ref[:, part] = left
        term = mm3(left, split(test[part, :]), ((1,), (0,)))
        total = term if total is None else total + term
    half = total.shape[0] // 2
    first = lax.axis_index(axis) & 1
    low, high_ = total[:half], total[half:]
    mine_ref[...] = jnp.where(first == 0, low, high_)
    other_ref[...] = jnp.where(first == 0, high_, low)


def sketch_parts(snapshot, test_matrix, axis):
    points, depth = snapshot.shape
    width = test_matrix.shape[1]
    chunks = 8
    half = array((points // 2, width))
    return call(
        functools.partial(sketch_kernel, axis),
        (half, half, array(snapshot.shape, BF16), array(snapshot.shape, BF16)),
        pltpu.with_memory_space_constraint(snapshot, pltpu.HBM),
        pltpu.with_memory_space_constraint(test_matrix, pltpu.HBM),
        specs=[ANY, ANY],
        scratch=[
            pltpu.VMEM(snapshot.shape, F32),
            pltpu.VMEM(test_matrix.shape, F32),
            pltpu.SemaphoreType.DMA((2, chunks)),
        ],
        flops=6 * points * depth * width,
        vmem=24,
    )


def swap(value, axis, mask):
    return lax.ppermute(value, axis, [(i, i ^ mask) for i in range(lax.axis_size(axis))])


def first_bit(axis):
    return lax.axis_index(axis) & 1


def ordered(axis, mine, other):
    low = first_bit(axis) == 0
    return jnp.where(low, mine, other), jnp.where(low, other, mine)


def strip_kernel(axis, mine_ref, other_ref, out_ref, scratch):
    half = mine_ref.shape[0]
    bit = first_bit(axis)
    scratch[pl.ds(pl.multiple_of(bit * half, half), half), :] = mine_ref[...]
    scratch[pl.ds(pl.multiple_of((1 - bit) * half, half), half), :] = other_ref[...]
    width = out_ref.shape[1]
    left = scratch[:, pl.ds(pl.multiple_of(bit * width, width), width)]
    out_ref[:width, :] = mm(left, left, ((0,), (0,)))
    cross = mm(scratch[:, :width], scratch[:, width:], ((0,), (0,)))
    out_ref[width:, :] = jnp.where(bit == 0, cross[: width // 2], cross[width // 2 :])


def gram_part(mine, other, axis):
    half, width = mine.shape
    block = width // 2
    (out,) = call(
        functools.partial(strip_kernel, axis),
        [array((block + block // 2, block))],
        mine,
        other,
        scratch=[pltpu.VMEM((2 * half, width), F32)],
        flops=6 * half * width * width,
    )
    return out


def gram_upper(axis, mine, other):
    first, second = ordered(axis, mine, other)
    block = first.shape[1]
    cross = jnp.concatenate([first[block:], second[block:]])
    above = jnp.concatenate([first[:block], cross], axis=1)
    below = jnp.concatenate([jnp.zeros_like(cross), second[:block]], axis=1)
    return jnp.concatenate([above, below])


class Ring:
    def __init__(self, axis):
        self.axis = axis
        self.length = lax.axis_size(axis)

    def slab(self, ahead):
        index = lax.axis_index(self.axis)
        place = index >> 1
        here = jnp.where((index & 1) == 0, place, self.length - 1 - place)
        return lax.rem(here + (ahead % self.length), self.length)

    def row(self, position):
        n = self.length
        position %= n
        return 2 * position if 2 * position < n else 2 * (n - 1 - position) + 1

    def send(self, value, way):
        pairs = [(self.row(p), self.row(p + way)) for p in range(self.length)]
        return lax.ppermute(value, self.axis, pairs)


def product_kernel(ring, axis, aheads, first, *refs):
    if first:
        mine_ref, other_ref, top_ref, rest_ref, stop_ref, srest_ref, *outs = refs
        half = mine_ref.shape[0]
        bit = first_bit(axis)
        for ref, at in ((mine_ref, bit), (other_ref, 1 - bit)):
            where = pl.ds(pl.multiple_of(at * half, half), half)
            stop_ref[where, :], srest_ref[where, :] = split(ref[...])
    else:
        stop_ref, srest_ref, top_ref, rest_ref, *outs = refs
    right = (stop_ref[...], srest_ref[...])
    for ahead, out in zip(aheads, outs):
        size = out.shape[0]
        at = pl.ds(pl.multiple_of(ring.slab(ahead) * size, size), size)
        out[...] = mm3((top_ref[:, at], rest_ref[:, at]), right, ((0,), (0,)))


def products(ring, axis, aheads, first, one, two, top, rest):
    points, columns = top.shape
    width = one.shape[1]
    size = columns // ring.length
    outs = [array((size, width))] * len(aheads)
    if first:
        outs = [array((points, width), BF16)] * 2 + outs
    return call(
        functools.partial(product_kernel, ring, axis, aheads, first),
        outs,
        one,
        two,
        top,
        rest,
        flops=6 * points * width * size * len(aheads),
        vmem=12,
    )


def final_kernel(ring, places, panels, *refs):
    count = len(places)
    lower = refs[:panels]
    pieces, refs = refs[panels : panels + count], refs[panels + count :]
    out_any, held, sems = refs[-3:]
    n = held.shape[2]
    size = out_any.shape[0] // ring.length
    right = split(jnp.concatenate([ref[:, n:] for ref in lower]))
    copies = []
    for i, ((ahead, offset), piece) in enumerate(zip(places, pieces)):
        rows = piece.shape[0]
        held[i, :rows] = mm3(split(piece[...]), right, ((1,), (1,)))
        at = pl.ds(pl.multiple_of(ring.slab(ahead) * size + offset, rows), rows)
        copy = pltpu.make_async_copy(held.at[i, pl.ds(0, rows)], out_any.at[at], sems.at[i])
        copy.start()
        copies.append(copy)
    for copy in copies:
        copy.wait()


def final(ring, pieces, panels, size, before=None):
    width = panels[0].shape[1] // 2
    args = [*panels, *pieces.values()]
    specs = [VMEM] * len(args)
    more = {}
    if before is not None:
        more["input_output_aliases"] = {len(args): 0}
        args.append(before)
        specs.append(ANY)
    count = len(pieces)
    (out,) = call(
        functools.partial(final_kernel, ring, tuple(pieces), len(panels)),
        [array((size * ring.length, width))],
        *args,
        specs=specs,
        out_specs=(ANY,),
        scratch=[pltpu.VMEM((count, size, width), F32), pltpu.SemaphoreType.DMA((count,))],
        flops=6 * sum(p.shape[0] for p in pieces.values()) * width * width,
        **more,
    )
    return out


def body(snapshot, test_matrix):
    return steps(snapshot, test_matrix)


def steps(snapshot, test_matrix):
    mine, other, top, rest = sketch_parts(snapshot, test_matrix, "cols")
    columns = lax.axis_size("cols")
    mine = mine + swap(other, "cols", 1)
    mask = 2
    while mask < columns:
        mine = mine + swap(mine, "cols", mask)
        mask *= 2
    other = swap(mine, "cols", 1)

    ring = Ring("rows")
    far = ring.length // 2
    stop, srest, part = products(ring, "cols", [far], True, mine, other, top, rest)
    size = part.shape[0]
    half = size // 2
    right, left = part[:half], part[half:]
    right = ring.send(right, 1)
    left = ring.send(left, -1)
    strip = gram_part(mine, other, "cols")
    step = 1
    while step < ring.length:
        strip = strip + swap(strip, "rows", step)
        step *= 2
    gram = gram_upper("cols", strip, swap(strip, "cols", 1))
    aheads = [sign * d for d in range(far - 1, 0, -1) for sign in (1, -1)] + [0]
    parts = products(ring, "cols", aheads, False, stop, srest, top, rest)
    parts = dict(zip(aheads, parts))
    for d in range(far - 1, 0, -1):
        if d == far - 1:
            right = jnp.pad(right, ((0, half), (0, 0)))
            left = jnp.pad(left, ((half, 0), (0, 0)))
        right = ring.send(parts[d] + right, 1)
        left = ring.send(parts[-d] + left, -1)
    own = parts[0] + (right + left)
    panels = []
    while len(panels) * PANEL < gram.shape[0]:
        panels.append(factor_rows(gram, panels))
    early, late = {(0, 0): own}, {}
    right = left = own
    for d in range(1, far + 1):
        if d == far:
            right, left = right[:half], left[half:]
        right = ring.send(right, 1)
        left = ring.send(left, -1)
        held = early if d < far else late
        held[-d, 0] = right
        held[d, half if d == far else 0] = left
    out = final(ring, early, panels, size)
    projected = final(ring, late, panels, size, out)
    total = snapshot.shape[0] * lax.axis_size("rows")
    return (projected, upper_part(panels) / jnp.sqrt(jnp.float32(total)))


def plain_body(snapshot, test_matrix):
    sketch = lax.psum(mm(snapshot, test_matrix, ((1,), (0,))), "cols")
    gram = lax.psum(mm(sketch, sketch, ((0,), (0,))), "rows")
    panels = []
    while len(panels) * PANEL < gram.shape[0]:
        panels.append(factor_rows(gram, panels))
    product = lax.psum(mm(snapshot, sketch, ((0,), (0,))), "rows")
    total = snapshot.shape[0] * lax.axis_size("rows")
    projected = mm(product, lower_part(panels), ((1,), (1,)))
    return (projected, upper_part(panels) / jnp.sqrt(jnp.float32(total)))


def solution(mesh):
    rows = mesh.shape["rows"]
    ring = rows == 8
    return jax.shard_map(
        body if ring else plain_body,
        mesh=mesh,
        in_specs=(P("rows", "cols"), P("cols", None)),
        out_specs=(P("cols", None), P()),
        check_vma=False,
    )
```

```python
import functools

import jax
import jax.numpy as jnp
from jax import lax
from jax.experimental import pallas as pl
from jax.experimental.pallas import tpu as pltpu
from jax.sharding import PartitionSpec as P


high = lax.Precision.HIGHEST
VMEM = pl.BlockSpec(memory_space=pltpu.VMEM)
ANY = pl.BlockSpec(memory_space=pltpu.HBM)
F32, BF16 = jnp.float32, jnp.bfloat16
MIB = 1 << 20
PANEL = 32


def mm(left, right, dims, precision=high):
    return lax.dot_general(
        left, right, (dims, ((), ())), precision=precision, preferred_element_type=F32
    )


def split(value):
    top = value.astype(BF16)
    return top, (value - top.astype(F32)).astype(BF16)


def mm3(left, right, dims):
    (at_left,), (at_right,) = dims
    return lax.dot_general(
        jnp.concatenate([left[0], left[0], left[1]], axis=at_left),
        jnp.concatenate([right[0], right[1], right[0]], axis=at_right),
        (dims, ((), ())),
        preferred_element_type=F32,
    )


def array(shape, dtype=F32):
    return jax.ShapeDtypeStruct(shape, dtype)


def call(kernel, outs, *args, specs=None, out_specs=None, scratch=(), flops=0, vmem=8, **more):
    outs = tuple(outs)
    return pl.pallas_call(
        kernel,
        out_shape=outs,
        in_specs=specs or [VMEM] * len(args),
        out_specs=out_specs or (VMEM,) * len(outs),
        scratch_shapes=list(scratch),
        compiler_params=pltpu.CompilerParams(vmem_limit_bytes=vmem * MIB),
        cost_estimate=pl.CostEstimate(
            flops=flops,
            bytes_accessed=sum(a.size * a.dtype.itemsize for a in args),
            transcendentals=0,
        ),
        **more,
    )(*args)


def factor_kernel(block, top, gram_ref, *refs):
    *above, out_ref, part = refs
    panel, n = out_ref.shape[0], gram_ref.shape[0]
    lanes, group = 128, 8
    row = lax.broadcasted_iota(jnp.int32, (panel, n), 0)
    col = lax.broadcasted_iota(jnp.int32, (panel, n), 1)
    low = top // lanes * lanes
    high_ = n + pl.cdiv(top + panel, lanes) * lanes
    width = high_ - low
    sub = lax.broadcasted_iota(jnp.int32, (group, width), 0)

    def wide(v):
        return jnp.concatenate([v] * (width // lanes), axis=1)

    eye = jnp.where(row + top == col, 1.0, 0.0).astype(F32)
    rest = jnp.concatenate([gram_ref[top : top + panel, :], eye], axis=1)[:, low:high_]
    for ref in above:
        rest = rest - mm(ref[:, top : top + panel], ref[:, low:high_], ((0,), (0,)))
    part[:, low:high_] = rest
    if low > 0:
        out_ref[:, :low] = jnp.zeros((panel, low), F32)
    if high_ < 2 * n:
        out_ref[:, high_:] = jnp.zeros((panel, 2 * n - high_), F32)
    for inner in range(0, panel, block):
        k = top + inner - low
        d, rows = {}, []
        for g in range(0, block, group):
            rows.append(part[inner + g : inner + g + group, low:high_])
            for j in range(g, block):
                c = jnp.broadcast_to(rows[-1][:, k + j : k + j + 1], (group, lanes))
                for i in range(g, min(g + group, j + 1)):
                    d[i, j] = jnp.broadcast_to(c[i - g : i - g + 1, :], (group, lanes))
        scale = []
        for i in range(block):
            scale.append(lax.rsqrt(d[i, i]))
            for j in range(i + 1, block):
                d[i, j] = d[i, j] * scale[i]
            for j in range(i + 1, block):
                for l in range(j, block):
                    d[j, l] = d[j, l] - d[i, j] * d[i, l]
        done, solved = [], []
        for i in range(block):
            g, at = divmod(i, group)
            if at == 0:
                solved.append(jnp.zeros((group, width), F32))
            line = jnp.broadcast_to(rows[g][at : at + 1, :], (group, width))
            for m in range(i):
                line = line - wide(d[m, i]) * done[m]
            line = line * wide(scale[i])
            done.append(line)
            solved[g] = jnp.where(sub == at, line, solved[g])
        solved = jnp.concatenate(solved)
        out_ref[inner : inner + block, low:high_] = solved
        if inner + block < panel:
            part[inner + block :, low:high_] -= mm(
                solved[:, k + block : top + panel - low], solved, ((0,), (0,))
            )


def factor_rows(gram, above):
    n = gram.shape[0]
    panel = min(n, PANEL)
    top = panel * len(above)
    (rows,) = call(
        functools.partial(factor_kernel, 16, top),
        [array((panel, 2 * n))],
        gram,
        *above,
        scratch=[pltpu.VMEM((panel, 2 * n), F32)],
        flops=12 * n * n * panel,
    )
    return rows


def upper_part(panels):
    n = panels[0].shape[1] // 2
    whole = jnp.concatenate([p[:, :n] for p in panels])
    return jnp.triu(whole)


def lower_part(panels):
    n = panels[0].shape[1] // 2
    return jnp.concatenate([p[:, n:] for p in panels])


def sketch_kernel(axis, snap_any, test_any, mine_ref, other_ref, top_ref, rest_ref, snap, test, sems):
    depth = snap.shape[1]
    chunks = sems.shape[1]
    size = depth // chunks
    copies = []
    for c in range(chunks):
        part = pl.ds(c * size, size)
        copies.append(
            (
                pltpu.make_async_copy(snap_any.at[:, part], snap.at[:, part], sems.at[0, c]),
                pltpu.make_async_copy(test_any.at[part], test.at[part], sems.at[1, c]),
            )
        )
    for c, (a, b) in enumerate(copies):
        b.start(priority=int(c > 0))
        a.start(priority=int(c > 0))
    total = None
    for c, (a, b) in enumerate(copies):
        b.wait()
        a.wait()
        part = slice(c * size, (c + 1) * size)
        left = split(snap[:, part])
        top_ref[:, part], rest_ref[:, part] = left
        term = mm3(left, split(test[part, :]), ((1,), (0,)))
        total = term if total is None else total + term
    half = total.shape[0] // 2
    first = lax.axis_index(axis) & 1
    low, high_ = total[:half], total[half:]
    mine_ref[...] = jnp.where(first == 0, low, high_)
    other_ref[...] = jnp.where(first == 0, high_, low)


def sketch_parts(snapshot, test_matrix, axis):
    points, depth = snapshot.shape
    width = test_matrix.shape[1]
    chunks = 2
    half = array((points // 2, width))
    return call(
        functools.partial(sketch_kernel, axis),
        (half, half, array(snapshot.shape, BF16), array(snapshot.shape, BF16)),
        pltpu.with_memory_space_constraint(snapshot, pltpu.HBM),
        pltpu.with_memory_space_constraint(test_matrix, pltpu.HBM),
        specs=[ANY, ANY],
        scratch=[
            pltpu.VMEM(snapshot.shape, F32),
            pltpu.VMEM(test_matrix.shape, F32),
            pltpu.SemaphoreType.DMA((2, chunks)),
        ],
        flops=6 * points * depth * width,
        vmem=24,
    )


def swap(value, axis, mask):
    return lax.ppermute(value, axis, [(i, i ^ mask) for i in range(lax.axis_size(axis))])


def first_bit(axis):
    return lax.axis_index(axis) & 1


def join(bit, mine, other):
    low = bit == 0
    return jnp.concatenate([jnp.where(low, mine, other), jnp.where(low, other, mine)])


def ordered(axis, mine, other):
    low = first_bit(axis) == 0
    return jnp.where(low, mine, other), jnp.where(low, other, mine)


def strip_kernel(axis, mine_ref, other_ref, out_ref, scratch):
    half = mine_ref.shape[0]
    bit = first_bit(axis)
    scratch[pl.ds(pl.multiple_of(bit * half, half), half), :] = mine_ref[...]
    scratch[pl.ds(pl.multiple_of((1 - bit) * half, half), half), :] = other_ref[...]
    width = out_ref.shape[1]
    left = scratch[:, pl.ds(pl.multiple_of(bit * width, width), width)]
    cross = mm(scratch[:, :width], scratch[:, width:], ((0,), (0,)))
    below = jnp.where(bit == 0, cross[: width // 2], cross[width // 2 :])
    whole = jnp.concatenate([mm(left, left, ((0,), (0,))), below])
    share = out_ref.shape[0]
    out_ref[...] = whole[:share]
    for n in range(1, whole.shape[0] // share):

        @pl.when((lax.axis_index(axis) >> 1) % (whole.shape[0] // share) == n)
        def _():
            out_ref[...] = whole[n * share : (n + 1) * share]


def gram_part(mine, other, axis):
    half, width = mine.shape
    block = width // 2
    shares = 2 if lax.axis_size(axis) % 4 == 0 else 1
    (out,) = call(
        functools.partial(strip_kernel, axis),
        [array(((block + block // 2) // shares, block))],
        mine,
        other,
        scratch=[pltpu.VMEM((2 * half, width), F32)],
        flops=6 * half * width * width,
    )
    return out


def gram_upper(axis, mine, other):
    first, second = ordered(axis, mine, other)
    block = first.shape[1]
    cross = jnp.concatenate([first[block:], second[block:]])
    above = jnp.concatenate([first[:block], cross], axis=1)
    below = jnp.concatenate([jnp.zeros_like(cross), second[:block]], axis=1)
    return jnp.concatenate([above, below])


class Ring:
    def __init__(self, axis):
        self.axis = axis
        self.length = lax.axis_size(axis)

    def slab(self, ahead):
        index = lax.axis_index(self.axis)
        place = index >> 1
        here = jnp.where((index & 1) == 0, place, self.length - 1 - place)
        return lax.rem(here + (ahead % self.length), self.length)

    def row(self, position):
        n = self.length
        position %= n
        return 2 * position if 2 * position < n else 2 * (n - 1 - position) + 1

    def send(self, value, way):
        pairs = [(self.row(p), self.row(p + way)) for p in range(self.length)]
        return lax.ppermute(value, self.axis, pairs)


def product_kernel(ring, axis, aheads, first, *refs):
    if first:
        mine_ref, other_ref, top_ref, rest_ref, stop_ref, srest_ref, *outs = refs
        half = mine_ref.shape[0]
        bit = first_bit(axis)
        for ref, at in ((mine_ref, bit), (other_ref, 1 - bit)):
            where = pl.ds(pl.multiple_of(at * half, half), half)
            stop_ref[where, :], srest_ref[where, :] = split(ref[...])
    else:
        stop_ref, srest_ref, top_ref, rest_ref, *outs = refs
    right = (stop_ref[...], srest_ref[...])
    for ahead, out in zip(aheads, outs):
        size = out.shape[0]
        at = pl.ds(pl.multiple_of(ring.slab(ahead) * size, size), size)
        out[...] = mm3((top_ref[:, at], rest_ref[:, at]), right, ((0,), (0,)))


def products(ring, axis, aheads, first, one, two, top, rest):
    points, columns = top.shape
    width = one.shape[1]
    size = columns // ring.length
    outs = [array((size, width))] * len(aheads)
    if first:
        outs = [array((points, width), BF16)] * 2 + outs
    return call(
        functools.partial(product_kernel, ring, axis, aheads, first),
        outs,
        one,
        two,
        top,
        rest,
        flops=6 * points * width * size * len(aheads),
        vmem=12,
    )


def final_kernel(ring, places, panels, *refs):
    count = len(places)
    lower = refs[:panels]
    pieces, refs = refs[panels : panels + count], refs[panels + count :]
    out_any, held, sems = refs[-3:]
    n = held.shape[2]
    size = out_any.shape[0] // ring.length
    right = split(jnp.concatenate([ref[:, n:] for ref in lower]))
    copies = []
    for i, ((ahead, offset), piece) in enumerate(zip(places, pieces)):
        rows = piece.shape[0]
        held[i, :rows] = mm3(split(piece[...]), right, ((1,), (1,)))
        at = pl.ds(pl.multiple_of(ring.slab(ahead) * size + offset, rows), rows)
        copy = pltpu.make_async_copy(held.at[i, pl.ds(0, rows)], out_any.at[at], sems.at[i])
        copy.start()
        copies.append(copy)
    for copy in copies:
        copy.wait()


def final(ring, pieces, panels, size, before=None):
    width = panels[0].shape[1] // 2
    args = [*panels, *pieces.values()]
    specs = [VMEM] * len(args)
    more = {}
    if before is not None:
        more["input_output_aliases"] = {len(args): 0}
        args.append(before)
        specs.append(ANY)
    count = len(pieces)
    (out,) = call(
        functools.partial(final_kernel, ring, tuple(pieces), len(panels)),
        [array((size * ring.length, width))],
        *args,
        specs=specs,
        out_specs=(ANY,),
        scratch=[pltpu.VMEM((count, size, width), F32), pltpu.SemaphoreType.DMA((count,))],
        flops=6 * sum(p.shape[0] for p in pieces.values()) * width * width,
        **more,
    )
    return out


def body(snapshot, test_matrix):
    rows, columns = lax.axis_size("rows"), lax.axis_size("cols")
    whole = snapshot.shape[1] % (128 * rows) == 0 and test_matrix.shape[1] % 256 == 0
    powers = rows & (rows - 1) == 0 and columns & (columns - 1) == 0
    if not (whole and powers and rows > 2 and columns > 1):
        return plain_body(snapshot, test_matrix)
    return steps(snapshot, test_matrix)


def steps(snapshot, test_matrix):
    mine, other, top, rest = sketch_parts(snapshot, test_matrix, "cols")
    columns = lax.axis_size("cols")
    mine = mine + swap(other, "cols", 1)
    mask = 2
    while mask < columns:
        mine = mine + swap(mine, "cols", mask)
        mask *= 2
    other = swap(mine, "cols", 1)

    ring = Ring("rows")
    far = ring.length // 2
    stop, srest, part = products(ring, "cols", [far], True, mine, other, top, rest)
    size = part.shape[0]
    half = size // 2
    right, left = part[:half], part[half:]
    right = ring.send(right, 1)
    left = ring.send(left, -1)
    strip = gram_part(mine, other, "cols")
    step = 1
    while step < ring.length:
        strip = strip + swap(strip, "rows", step)
        step *= 2
    if columns % 4 == 0:
        strip = join((lax.axis_index("cols") >> 1) & 1, strip, swap(strip, "cols", 2))
    gram = gram_upper("cols", strip, swap(strip, "cols", 1))
    aheads = [sign * d for d in range(far - 1, 0, -1) for sign in (1, -1)] + [0]
    parts = products(ring, "cols", aheads[:2], False, stop, srest, top, rest)
    parts += products(ring, "cols", aheads[2:], False, stop, srest, top, rest)
    parts = dict(zip(aheads, parts))
    for d in range(far - 1, 0, -1):
        if d == far - 1:
            right = jnp.pad(right, ((0, half), (0, 0)))
            left = jnp.pad(left, ((half, 0), (0, 0)))
        right = ring.send(parts[d] + right, 1)
        left = ring.send(parts[-d] + left, -1)
    own = parts[0] + (right + left)
    panels = []
    while len(panels) * PANEL < gram.shape[0]:
        panels.append(factor_rows(gram, panels))
    early, late = {(0, 0): own}, {}
    right = left = own
    for d in range(1, far + 1):
        if d == far:
            right, left = right[:half], left[half:]
        right = ring.send(right, 1)
        left = ring.send(left, -1)
        held = early if d < far else late
        held[-d, 0] = right
        held[d, half if d == far else 0] = left
    out = final(ring, early, panels, size)
    projected = final(ring, late, panels, size, out)
    total = snapshot.shape[0] * lax.axis_size("rows")
    return (projected, upper_part(panels) / jnp.sqrt(jnp.float32(total)))


def plain_body(snapshot, test_matrix):
    sketch = lax.psum(mm(snapshot, test_matrix, ((1,), (0,))), "cols")
    gram = lax.psum(mm(sketch, sketch, ((0,), (0,))), "rows")
    panels = []
    while len(panels) * PANEL < gram.shape[0]:
        panels.append(factor_rows(gram, panels))
    product = lax.psum(mm(snapshot, sketch, ((0,), (0,))), "rows")
    total = snapshot.shape[0] * lax.axis_size("rows")
    projected = mm(product, lower_part(panels), ((1,), (1,)))
    return (projected, upper_part(panels) / jnp.sqrt(jnp.float32(total)))


def solution(mesh):
    return jax.shard_map(
        body,
        mesh=mesh,
        in_specs=(P("rows", "cols"), P("cols", None)),
        out_specs=(P("cols", None), P()),
        check_vma=False,
    )
```

```python
import functools

import jax
import jax.numpy as jnp
from jax import lax
from jax.experimental import pallas as pl
from jax.experimental.pallas import tpu as pltpu
from jax.sharding import PartitionSpec as P


high = lax.Precision.HIGHEST
VMEM = pl.BlockSpec(memory_space=pltpu.VMEM)
ANY = pl.BlockSpec(memory_space=pltpu.HBM)
F32, BF16 = jnp.float32, jnp.bfloat16
MIB = 1 << 20
PANEL = 32


def mm(left, right, dims, precision=high):
    return lax.dot_general(
        left, right, (dims, ((), ())), precision=precision, preferred_element_type=F32
    )


def split(value):
    top = value.astype(BF16)
    return top, (value - top.astype(F32)).astype(BF16)


def mm3(left, right, dims):
    (at_left,), (at_right,) = dims
    return lax.dot_general(
        jnp.concatenate([left[0], left[0], left[1]], axis=at_left),
        jnp.concatenate([right[0], right[1], right[0]], axis=at_right),
        (dims, ((), ())),
        preferred_element_type=F32,
    )


def array(shape, dtype=F32):
    return jax.ShapeDtypeStruct(shape, dtype)


def call(kernel, outs, *args, specs=None, out_specs=None, scratch=(), flops=0, vmem=8, **more):
    outs = tuple(outs)
    return pl.pallas_call(
        kernel,
        out_shape=outs,
        in_specs=specs or [VMEM] * len(args),
        out_specs=out_specs or (VMEM,) * len(outs),
        scratch_shapes=list(scratch),
        compiler_params=pltpu.CompilerParams(vmem_limit_bytes=vmem * MIB),
        cost_estimate=pl.CostEstimate(
            flops=flops,
            bytes_accessed=sum(a.size * a.dtype.itemsize for a in args),
            transcendentals=0,
        ),
        **more,
    )(*args)


def factor_kernel(block, top, gram_ref, *refs):
    *above, out_ref, part = refs
    panel, n = out_ref.shape[0], gram_ref.shape[0]
    lanes, group = 128, 8
    row = lax.broadcasted_iota(jnp.int32, (panel, n), 0)
    col = lax.broadcasted_iota(jnp.int32, (panel, n), 1)
    low = top // lanes * lanes
    high_ = n + pl.cdiv(top + panel, lanes) * lanes
    width = high_ - low
    sub = lax.broadcasted_iota(jnp.int32, (group, width), 0)

    def wide(v):
        return jnp.concatenate([v] * (width // lanes), axis=1)

    eye = jnp.where(row + top == col, 1.0, 0.0).astype(F32)
    rest = jnp.concatenate([gram_ref[top : top + panel, :], eye], axis=1)[:, low:high_]
    for ref in above:
        rest = rest - mm(ref[:, top : top + panel], ref[:, low:high_], ((0,), (0,)))
    part[:, low:high_] = rest
    if low > 0:
        out_ref[:, :low] = jnp.zeros((panel, low), F32)
    if high_ < 2 * n:
        out_ref[:, high_:] = jnp.zeros((panel, 2 * n - high_), F32)
    for inner in range(0, panel, block):
        k = top + inner - low
        d, rows = {}, []
        for g in range(0, block, group):
            rows.append(part[inner + g : inner + g + group, low:high_])
            for j in range(g, block):
                c = jnp.broadcast_to(rows[-1][:, k + j : k + j + 1], (group, lanes))
                for i in range(g, min(g + group, j + 1)):
                    d[i, j] = jnp.broadcast_to(c[i - g : i - g + 1, :], (group, lanes))
        scale = []
        for i in range(block):
            scale.append(lax.rsqrt(d[i, i]))
            for j in range(i + 1, block):
                d[i, j] = d[i, j] * scale[i]
            for j in range(i + 1, block):
                for l in range(j, block):
                    d[j, l] = d[j, l] - d[i, j] * d[i, l]
        done, solved = [], []
        for i in range(block):
            g, at = divmod(i, group)
            if at == 0:
                solved.append(jnp.zeros((group, width), F32))
            line = jnp.broadcast_to(rows[g][at : at + 1, :], (group, width))
            for m in range(i):
                line = line - wide(d[m, i]) * done[m]
            line = line * wide(scale[i])
            done.append(line)
            solved[g] = jnp.where(sub == at, line, solved[g])
        solved = jnp.concatenate(solved)
        out_ref[inner : inner + block, low:high_] = solved
        if inner + block < panel:
            part[inner + block :, low:high_] -= mm(
                solved[:, k + block : top + panel - low], solved, ((0,), (0,))
            )


def factor_rows(gram, above):
    n = gram.shape[0]
    panel = min(n, PANEL)
    top = panel * len(above)
    (rows,) = call(
        functools.partial(factor_kernel, 16, top),
        [array((panel, 2 * n))],
        gram,
        *above,
        scratch=[pltpu.VMEM((panel, 2 * n), F32)],
        flops=12 * n * n * panel,
    )
    return rows


def upper_part(panels):
    n = panels[0].shape[1] // 2
    whole = jnp.concatenate([p[:, :n] for p in panels])
    return jnp.triu(whole)


def lower_part(panels):
    n = panels[0].shape[1] // 2
    return jnp.concatenate([p[:, n:] for p in panels])


def sketch_kernel(axis, snap_any, test_any, mine_ref, other_ref, top_ref, rest_ref, snap, test, sems):
    depth = snap.shape[1]
    chunks = sems.shape[1]
    size = depth // chunks
    copies = []
    for c in range(chunks):
        part = pl.ds(c * size, size)
        copies.append(
            (
                pltpu.make_async_copy(snap_any.at[:, part], snap.at[:, part], sems.at[0, c]),
                pltpu.make_async_copy(test_any.at[part], test.at[part], sems.at[1, c]),
            )
        )
    for c, (a, b) in enumerate(copies):
        b.start(priority=int(c > 0))
        a.start(priority=int(c > 0))
    total = None
    for c, (a, b) in enumerate(copies):
        b.wait()
        a.wait()
        part = slice(c * size, (c + 1) * size)
        left = split(snap[:, part])
        top_ref[:, part], rest_ref[:, part] = left
        term = mm3(left, split(test[part, :]), ((1,), (0,)))
        total = term if total is None else total + term
    half = total.shape[0] // 2
    first = lax.axis_index(axis) & 1
    low, high_ = total[:half], total[half:]
    mine_ref[...] = jnp.where(first == 0, low, high_)
    other_ref[...] = jnp.where(first == 0, high_, low)


def sketch_parts(snapshot, test_matrix, axis):
    points, depth = snapshot.shape
    width = test_matrix.shape[1]
    chunks = 2
    half = array((points // 2, width))
    return call(
        functools.partial(sketch_kernel, axis),
        (half, half, array(snapshot.shape, BF16), array(snapshot.shape, BF16)),
        pltpu.with_memory_space_constraint(snapshot, pltpu.HBM),
        pltpu.with_memory_space_constraint(test_matrix, pltpu.HBM),
        specs=[ANY, ANY],
        scratch=[
            pltpu.VMEM(snapshot.shape, F32),
            pltpu.VMEM(test_matrix.shape, F32),
            pltpu.SemaphoreType.DMA((2, chunks)),
        ],
        flops=6 * points * depth * width,
        vmem=24,
    )


def swap(value, axis, mask):
    return lax.ppermute(value, axis, [(i, i ^ mask) for i in range(lax.axis_size(axis))])


def first_bit(axis):
    return lax.axis_index(axis) & 1


def join(bit, mine, other):
    low = bit == 0
    return jnp.concatenate([jnp.where(low, mine, other), jnp.where(low, other, mine)])


def ordered(axis, mine, other):
    low = first_bit(axis) == 0
    return jnp.where(low, mine, other), jnp.where(low, other, mine)


def strip_kernel(axis, mine_ref, other_ref, out_ref, scratch):
    half = mine_ref.shape[0]
    bit = first_bit(axis)
    scratch[pl.ds(pl.multiple_of(bit * half, half), half), :] = mine_ref[...]
    scratch[pl.ds(pl.multiple_of((1 - bit) * half, half), half), :] = other_ref[...]
    width = out_ref.shape[1]
    left = scratch[:, pl.ds(pl.multiple_of(bit * width, width), width)]
    cross = mm(scratch[:, :width], scratch[:, width:], ((0,), (0,)))
    below = jnp.where(bit == 0, cross[: width // 2], cross[width // 2 :])
    whole = jnp.concatenate([mm(left, left, ((0,), (0,))), below])
    share = out_ref.shape[0]
    out_ref[...] = whole[:share]
    for n in range(1, whole.shape[0] // share):

        @pl.when((lax.axis_index(axis) >> 1) % (whole.shape[0] // share) == n)
        def _():
            out_ref[...] = whole[n * share : (n + 1) * share]


def gram_part(mine, other, axis):
    half, width = mine.shape
    block = width // 2
    shares = 2 if lax.axis_size(axis) % 4 == 0 else 1
    (out,) = call(
        functools.partial(strip_kernel, axis),
        [array(((block + block // 2) // shares, block))],
        mine,
        other,
        scratch=[pltpu.VMEM((2 * half, width), F32)],
        flops=6 * half * width * width,
    )
    return out


def gram_upper(axis, mine, other):
    first, second = ordered(axis, mine, other)
    block = first.shape[1]
    cross = jnp.concatenate([first[block:], second[block:]])
    above = jnp.concatenate([first[:block], cross], axis=1)
    below = jnp.concatenate([jnp.zeros_like(cross), second[:block]], axis=1)
    return jnp.concatenate([above, below])


class Ring:
    def __init__(self, axis):
        self.axis = axis
        self.length = lax.axis_size(axis)

    def slab(self, ahead):
        index = lax.axis_index(self.axis)
        place = index >> 1
        here = jnp.where((index & 1) == 0, place, self.length - 1 - place)
        return lax.rem(here + (ahead % self.length), self.length)

    def row(self, position):
        n = self.length
        position %= n
        return 2 * position if 2 * position < n else 2 * (n - 1 - position) + 1

    def send(self, value, way):
        pairs = [(self.row(p), self.row(p + way)) for p in range(self.length)]
        return lax.ppermute(value, self.axis, pairs)


def product_kernel(ring, axis, aheads, first, *refs):
    if first:
        mine_ref, other_ref, top_ref, rest_ref, stop_ref, srest_ref, *outs = refs
        half = mine_ref.shape[0]
        bit = first_bit(axis)
        for ref, at in ((mine_ref, bit), (other_ref, 1 - bit)):
            where = pl.ds(pl.multiple_of(at * half, half), half)
            stop_ref[where, :], srest_ref[where, :] = split(ref[...])
    else:
        stop_ref, srest_ref, top_ref, rest_ref, *outs = refs
    right = (stop_ref[...], srest_ref[...])
    for ahead, out in zip(aheads, outs):
        size = out.shape[0]
        at = pl.ds(pl.multiple_of(ring.slab(ahead) * size, size), size)
        out[...] = mm3((top_ref[:, at], rest_ref[:, at]), right, ((0,), (0,)))


def products(ring, axis, aheads, first, one, two, top, rest):
    points, columns = top.shape
    width = one.shape[1]
    size = columns // ring.length
    outs = [array((size, width))] * len(aheads)
    if first:
        outs = [array((points, width), BF16)] * 2 + outs
    return call(
        functools.partial(product_kernel, ring, axis, aheads, first),
        outs,
        one,
        two,
        top,
        rest,
        flops=6 * points * width * size * len(aheads),
        vmem=12,
    )


def final_kernel(ring, places, panels, *refs):
    count = len(places)
    lower = refs[:panels]
    pieces, refs = refs[panels : panels + count], refs[panels + count :]
    out_any, held, sems = refs[-3:]
    n = held.shape[2]
    size = out_any.shape[0] // ring.length
    right = split(jnp.concatenate([ref[:, n:] for ref in lower]))
    copies = []
    for i, ((ahead, offset), piece) in enumerate(zip(places, pieces)):
        rows = piece.shape[0]
        held[i, :rows] = mm3(split(piece[...]), right, ((1,), (1,)))
        at = pl.ds(pl.multiple_of(ring.slab(ahead) * size + offset, rows), rows)
        copy = pltpu.make_async_copy(held.at[i, pl.ds(0, rows)], out_any.at[at], sems.at[i])
        copy.start()
        copies.append(copy)
    for copy in copies:
        copy.wait()


def final(ring, pieces, panels, size, before=None):
    width = panels[0].shape[1] // 2
    args = [*panels, *pieces.values()]
    specs = [VMEM] * len(args)
    more = {}
    if before is not None:
        more["input_output_aliases"] = {len(args): 0}
        args.append(before)
        specs.append(ANY)
    count = len(pieces)
    (out,) = call(
        functools.partial(final_kernel, ring, tuple(pieces), len(panels)),
        [array((size * ring.length, width))],
        *args,
        specs=specs,
        out_specs=(ANY,),
        scratch=[pltpu.VMEM((count, size, width), F32), pltpu.SemaphoreType.DMA((count,))],
        flops=6 * sum(p.shape[0] for p in pieces.values()) * width * width,
        **more,
    )
    return out


def body(snapshot, test_matrix):
    rows, columns = lax.axis_size("rows"), lax.axis_size("cols")
    whole = snapshot.shape[1] % (128 * rows) == 0 and test_matrix.shape[1] % 256 == 0
    powers = rows & (rows - 1) == 0 and columns & (columns - 1) == 0
    if not (whole and powers and rows > 2 and columns > 1):
        return plain_body(snapshot, test_matrix)
    return steps(snapshot, test_matrix)


def steps(snapshot, test_matrix):
    mine, other, top, rest = sketch_parts(snapshot, test_matrix, "cols")
    columns = lax.axis_size("cols")
    mine = mine + swap(other, "cols", 1)
    mid = mine.shape[0] // 2
    mask = 2
    while mask < columns:
        pieces = [swap(mine[:mid], "cols", mask), swap(mine[mid:], "cols", mask)]
        pieces = [mine[:mid] + pieces[0], mine[mid:] + pieces[1]]
        mask *= 2
        if mask < columns:
            mine = jnp.concatenate(pieces)
    others = [swap(piece, "cols", 1) for piece in pieces]
    mine, other = jnp.concatenate(pieces), jnp.concatenate(others)

    ring = Ring("rows")
    far = ring.length // 2
    stop, srest, part = products(ring, "cols", [far], True, mine, other, top, rest)
    size = part.shape[0]
    half = size // 2
    right, left = part[:half], part[half:]
    right = ring.send(right, 1)
    left = ring.send(left, -1)
    strip = gram_part(mine, other, "cols")
    step = 1
    while step < ring.length:
        strip = strip + swap(strip, "rows", step)
        step *= 2
    if columns % 4 == 0:
        strip = join((lax.axis_index("cols") >> 1) & 1, strip, swap(strip, "cols", 2))
    gram = gram_upper("cols", strip, swap(strip, "cols", 1))
    aheads = [sign * d for d in range(far - 1, 0, -1) for sign in (1, -1)] + [0]
    parts = products(ring, "cols", aheads[:2], False, stop, srest, top, rest)
    parts += products(ring, "cols", aheads[2:], False, stop, srest, top, rest)
    parts = dict(zip(aheads, parts))
    for d in range(far - 1, 0, -1):
        if d == far - 1:
            right = jnp.pad(right, ((0, half), (0, 0)))
            left = jnp.pad(left, ((half, 0), (0, 0)))
        right = ring.send(parts[d] + right, 1)
        left = ring.send(parts[-d] + left, -1)
    own = parts[0] + (right + left)
    panels = []
    while len(panels) * PANEL < gram.shape[0]:
        panels.append(factor_rows(gram, panels))
    early, late = {(0, 0): own}, {}
    right = left = own
    for d in range(1, far + 1):
        if d == far:
            right, left = right[:half], left[half:]
        right = ring.send(right, 1)
        left = ring.send(left, -1)
        held = early if d < far else late
        held[-d, 0] = right
        held[d, half if d == far else 0] = left
    out = final(ring, early, panels, size)
    projected = final(ring, late, panels, size, out)
    total = snapshot.shape[0] * lax.axis_size("rows")
    return (projected, upper_part(panels) / jnp.sqrt(jnp.float32(total)))


def plain_body(snapshot, test_matrix):
    sketch = lax.psum(mm(snapshot, test_matrix, ((1,), (0,))), "cols")
    gram = lax.psum(mm(sketch, sketch, ((0,), (0,))), "rows")
    panels = []
    while len(panels) * PANEL < gram.shape[0]:
        panels.append(factor_rows(gram, panels))
    product = lax.psum(mm(snapshot, sketch, ((0,), (0,))), "rows")
    total = snapshot.shape[0] * lax.axis_size("rows")
    projected = mm(product, lower_part(panels), ((1,), (1,)))
    return (projected, upper_part(panels) / jnp.sqrt(jnp.float32(total)))


def solution(mesh):
    return jax.shard_map(
        body,
        mesh=mesh,
        in_specs=(P("rows", "cols"), P("cols", None)),
        out_specs=(P("cols", None), P()),
        check_vma=False,
    )
```

```python
import functools

import jax
import jax.numpy as jnp
from jax import lax
from jax.experimental import pallas as pl
from jax.experimental.pallas import tpu as pltpu
from jax.sharding import PartitionSpec as P


high = lax.Precision.HIGHEST
VMEM = pl.BlockSpec(memory_space=pltpu.VMEM)
ANY = pl.BlockSpec(memory_space=pltpu.HBM)
F32, BF16 = jnp.float32, jnp.bfloat16
MIB = 1 << 20
PANEL = 32
FIRST = 4


def mm(left, right, dims, precision=high):
    return lax.dot_general(
        left, right, (dims, ((), ())), precision=precision, preferred_element_type=F32
    )


def split(value):
    top = value.astype(BF16)
    return top, (value - top.astype(F32)).astype(BF16)


def mm3(left, right, dims):
    (at_left,), (at_right,) = dims
    return lax.dot_general(
        jnp.concatenate([left[0], left[0], left[1]], axis=at_left),
        jnp.concatenate([right[0], right[1], right[0]], axis=at_right),
        (dims, ((), ())),
        preferred_element_type=F32,
    )


def array(shape, dtype=F32):
    return jax.ShapeDtypeStruct(shape, dtype)


def call(kernel, outs, *args, specs=None, out_specs=None, scratch=(), flops=0, vmem=8, **more):
    outs = tuple(outs)
    return pl.pallas_call(
        kernel,
        out_shape=outs,
        in_specs=specs or [VMEM] * len(args),
        out_specs=out_specs or (VMEM,) * len(outs),
        scratch_shapes=list(scratch),
        compiler_params=pltpu.CompilerParams(vmem_limit_bytes=vmem * MIB),
        cost_estimate=pl.CostEstimate(
            flops=flops,
            bytes_accessed=sum(a.size * a.dtype.itemsize for a in args),
            transcendentals=0,
        ),
        **more,
    )(*args)


def factor_kernel(block, top, gram_ref, *refs):
    *above, out_ref, part = refs
    panel, n = out_ref.shape[0], gram_ref.shape[0]
    lanes, group = 128, 8
    row = lax.broadcasted_iota(jnp.int32, (panel, n), 0)
    col = lax.broadcasted_iota(jnp.int32, (panel, n), 1)
    low = top // lanes * lanes
    high_ = n + pl.cdiv(top + panel, lanes) * lanes
    width = high_ - low
    sub = lax.broadcasted_iota(jnp.int32, (group, width), 0)

    def wide(v):
        return jnp.concatenate([v] * (width // lanes), axis=1)

    eye = jnp.where(row + top == col, 1.0, 0.0).astype(F32)
    rest = jnp.concatenate([gram_ref[top : top + panel, :], eye], axis=1)[:, low:high_]
    for ref in above:
        rest = rest - mm(ref[:, top : top + panel], ref[:, low:high_], ((0,), (0,)))
    part[:, low:high_] = rest
    if low > 0:
        out_ref[:, :low] = jnp.zeros((panel, low), F32)
    if high_ < 2 * n:
        out_ref[:, high_:] = jnp.zeros((panel, 2 * n - high_), F32)
    for inner in range(0, panel, block):
        k = top + inner - low
        d, rows = {}, []
        for g in range(0, block, group):
            rows.append(part[inner + g : inner + g + group, low:high_])
            for j in range(g, block):
                c = jnp.broadcast_to(rows[-1][:, k + j : k + j + 1], (group, lanes))
                for i in range(g, min(g + group, j + 1)):
                    d[i, j] = jnp.broadcast_to(c[i - g : i - g + 1, :], (group, lanes))
        scale = []
        for i in range(block):
            scale.append(lax.rsqrt(d[i, i]))
            for j in range(i + 1, block):
                d[i, j] = d[i, j] * scale[i]
            for j in range(i + 1, block):
                for l in range(j, block):
                    d[j, l] = d[j, l] - d[i, j] * d[i, l]
        done, solved = [], []
        for i in range(block):
            g, at = divmod(i, group)
            if at == 0:
                solved.append(jnp.zeros((group, width), F32))
            line = jnp.broadcast_to(rows[g][at : at + 1, :], (group, width))
            for m in range(i):
                line = line - wide(d[m, i]) * done[m]
            line = line * wide(scale[i])
            done.append(line)
            solved[g] = jnp.where(sub == at, line, solved[g])
        solved = jnp.concatenate(solved)
        out_ref[inner : inner + block, low:high_] = solved
        if inner + block < panel:
            part[inner + block :, low:high_] -= mm(
                solved[:, k + block : top + panel - low], solved, ((0,), (0,))
            )


def factor_rows(gram, above):
    n = gram.shape[0]
    panel = min(n, PANEL)
    top = panel * len(above)
    (rows,) = call(
        functools.partial(factor_kernel, 16, top),
        [array((panel, 2 * n))],
        gram,
        *above,
        scratch=[pltpu.VMEM((panel, 2 * n), F32)],
        flops=12 * n * n * panel,
    )
    return rows


def upper_part(panels):
    n = panels[0].shape[1] // 2
    whole = jnp.concatenate([p[:, :n] for p in panels])
    return jnp.triu(whole)


def lower_part(panels):
    n = panels[0].shape[1] // 2
    return jnp.concatenate([p[:, n:] for p in panels])


def sketch_kernel(axis, snap_any, test_any, mine_ref, other_ref, top_ref, rest_ref, snap, test, sems):
    depth = snap.shape[1]
    first = depth * FIRST // 16
    parts = ((0, first), (first, depth - first))
    copies = []
    for c, (start, size) in enumerate(parts):
        part = pl.ds(start, size)
        copies.append(
            (
                pltpu.make_async_copy(snap_any.at[:, part], snap.at[:, part], sems.at[0, c]),
                pltpu.make_async_copy(test_any.at[part], test.at[part], sems.at[1, c]),
            )
        )
    for c, (a, b) in enumerate(copies):
        b.start(priority=int(c > 0))
        a.start(priority=int(c > 0))
    total = None
    for c, (a, b) in enumerate(copies):
        b.wait()
        a.wait()
        part = slice(parts[c][0], sum(parts[c]))
        left = split(snap[:, part])
        top_ref[:, part], rest_ref[:, part] = left
        term = mm3(left, split(test[part, :]), ((1,), (0,)))
        total = term if total is None else total + term
    half = total.shape[0] // 2
    first = lax.axis_index(axis) & 1
    low, high_ = total[:half], total[half:]
    mine_ref[...] = jnp.where(first == 0, low, high_)
    other_ref[...] = jnp.where(first == 0, high_, low)


def sketch_parts(snapshot, test_matrix, axis):
    points, depth = snapshot.shape
    width = test_matrix.shape[1]
    chunks = 2
    half = array((points // 2, width))
    return call(
        functools.partial(sketch_kernel, axis),
        (half, half, array(snapshot.shape, BF16), array(snapshot.shape, BF16)),
        pltpu.with_memory_space_constraint(snapshot, pltpu.HBM),
        pltpu.with_memory_space_constraint(test_matrix, pltpu.HBM),
        specs=[ANY, ANY],
        scratch=[
            pltpu.VMEM(snapshot.shape, F32),
            pltpu.VMEM(test_matrix.shape, F32),
            pltpu.SemaphoreType.DMA((2, chunks)),
        ],
        flops=6 * points * depth * width,
        vmem=24,
    )


def swap(value, axis, mask):
    return lax.ppermute(value, axis, [(i, i ^ mask) for i in range(lax.axis_size(axis))])


def first_bit(axis):
    return lax.axis_index(axis) & 1


def join(bit, mine, other):
    low = bit == 0
    return jnp.concatenate([jnp.where(low, mine, other), jnp.where(low, other, mine)])


def ordered(axis, mine, other):
    low = first_bit(axis) == 0
    return jnp.where(low, mine, other), jnp.where(low, other, mine)


def strip_kernel(axis, mine_ref, other_ref, out_ref, scratch):
    half = mine_ref.shape[0]
    bit = first_bit(axis)
    scratch[pl.ds(pl.multiple_of(bit * half, half), half), :] = mine_ref[...]
    scratch[pl.ds(pl.multiple_of((1 - bit) * half, half), half), :] = other_ref[...]
    width = out_ref.shape[1]
    left = scratch[:, pl.ds(pl.multiple_of(bit * width, width), width)]
    cross = mm(scratch[:, :width], scratch[:, width:], ((0,), (0,)))
    below = jnp.where(bit == 0, cross[: width // 2], cross[width // 2 :])
    whole = jnp.concatenate([mm(left, left, ((0,), (0,))), below])
    share = out_ref.shape[0]
    out_ref[...] = whole[:share]
    for n in range(1, whole.shape[0] // share):

        @pl.when((lax.axis_index(axis) >> 1) % (whole.shape[0] // share) == n)
        def _():
            out_ref[...] = whole[n * share : (n + 1) * share]


def gram_part(mine, other, axis):
    half, width = mine.shape
    block = width // 2
    shares = 2 if lax.axis_size(axis) % 4 == 0 else 1
    (out,) = call(
        functools.partial(strip_kernel, axis),
        [array(((block + block // 2) // shares, block))],
        mine,
        other,
        scratch=[pltpu.VMEM((2 * half, width), F32)],
        flops=6 * half * width * width,
    )
    return out


def gram_upper(axis, mine, other):
    first, second = ordered(axis, mine, other)
    block = first.shape[1]
    cross = jnp.concatenate([first[block:], second[block:]])
    above = jnp.concatenate([first[:block], cross], axis=1)
    below = jnp.concatenate([jnp.zeros_like(cross), second[:block]], axis=1)
    return jnp.concatenate([above, below])


class Ring:
    def __init__(self, axis):
        self.axis = axis
        self.length = lax.axis_size(axis)

    def slab(self, ahead):
        index = lax.axis_index(self.axis)
        place = index >> 1
        here = jnp.where((index & 1) == 0, place, self.length - 1 - place)
        return lax.rem(here + (ahead % self.length), self.length)

    def row(self, position):
        n = self.length
        position %= n
        return 2 * position if 2 * position < n else 2 * (n - 1 - position) + 1

    def send(self, value, way):
        pairs = [(self.row(p), self.row(p + way)) for p in range(self.length)]
        return lax.ppermute(value, self.axis, pairs)


def product_kernel(ring, axis, aheads, first, *refs):
    if first:
        mine_ref, other_ref, top_ref, rest_ref, stop_ref, srest_ref, *outs = refs
        half = mine_ref.shape[0]
        bit = first_bit(axis)
        for ref, at in ((mine_ref, bit), (other_ref, 1 - bit)):
            where = pl.ds(pl.multiple_of(at * half, half), half)
            stop_ref[where, :], srest_ref[where, :] = split(ref[...])
    else:
        stop_ref, srest_ref, top_ref, rest_ref, *outs = refs
    right = (stop_ref[...], srest_ref[...])
    for ahead, out in zip(aheads, outs):
        size = out.shape[0]
        at = pl.ds(pl.multiple_of(ring.slab(ahead) * size, size), size)
        out[...] = mm3((top_ref[:, at], rest_ref[:, at]), right, ((0,), (0,)))


def products(ring, axis, aheads, first, one, two, top, rest):
    points, columns = top.shape
    width = one.shape[1]
    size = columns // ring.length
    outs = [array((size, width))] * len(aheads)
    if first:
        outs = [array((points, width), BF16)] * 2 + outs
    return call(
        functools.partial(product_kernel, ring, axis, aheads, first),
        outs,
        one,
        two,
        top,
        rest,
        flops=6 * points * width * size * len(aheads),
        vmem=12,
    )


def final_kernel(ring, places, panels, *refs):
    count = len(places)
    lower = refs[:panels]
    pieces, refs = refs[panels : panels + count], refs[panels + count :]
    out_any, held, sems = refs[-3:]
    n = held.shape[2]
    size = out_any.shape[0] // ring.length
    right = split(jnp.concatenate([ref[:, n:] for ref in lower]))
    copies = []
    for i, ((ahead, offset), piece) in enumerate(zip(places, pieces)):
        rows = piece.shape[0]
        held[i, :rows] = mm3(split(piece[...]), right, ((1,), (1,)))
        at = pl.ds(pl.multiple_of(ring.slab(ahead) * size + offset, rows), rows)
        copy = pltpu.make_async_copy(held.at[i, pl.ds(0, rows)], out_any.at[at], sems.at[i])
        copy.start()
        copies.append(copy)
    for copy in copies:
        copy.wait()


def final(ring, pieces, panels, size, before=None):
    width = panels[0].shape[1] // 2
    args = [*panels, *pieces.values()]
    specs = [VMEM] * len(args)
    more = {}
    if before is not None:
        more["input_output_aliases"] = {len(args): 0}
        args.append(before)
        specs.append(ANY)
    count = len(pieces)
    (out,) = call(
        functools.partial(final_kernel, ring, tuple(pieces), len(panels)),
        [array((size * ring.length, width))],
        *args,
        specs=specs,
        out_specs=(ANY,),
        scratch=[pltpu.VMEM((count, size, width), F32), pltpu.SemaphoreType.DMA((count,))],
        flops=6 * sum(p.shape[0] for p in pieces.values()) * width * width,
        **more,
    )
    return out


def body(snapshot, test_matrix):
    rows, columns = lax.axis_size("rows"), lax.axis_size("cols")
    whole = snapshot.shape[1] % (128 * rows) == 0 and test_matrix.shape[1] % 256 == 0
    powers = rows & (rows - 1) == 0 and columns & (columns - 1) == 0
    if not (whole and powers and rows > 2 and columns > 1):
        return plain_body(snapshot, test_matrix)
    return steps(snapshot, test_matrix)


def steps(snapshot, test_matrix):
    mine, other, top, rest = sketch_parts(snapshot, test_matrix, "cols")
    columns = lax.axis_size("cols")
    mine = mine + swap(other, "cols", 1)
    mid = mine.shape[0] // 2
    mask = 2
    while mask < columns:
        pieces = [swap(mine[:mid], "cols", mask), swap(mine[mid:], "cols", mask)]
        pieces = [mine[:mid] + pieces[0], mine[mid:] + pieces[1]]
        mask *= 2
        if mask < columns:
            mine = jnp.concatenate(pieces)
    others = [swap(piece, "cols", 1) for piece in pieces]
    mine, other = jnp.concatenate(pieces), jnp.concatenate(others)

    ring = Ring("rows")
    far = ring.length // 2
    stop, srest, part = products(ring, "cols", [far], True, mine, other, top, rest)
    size = part.shape[0]
    half = size // 2
    right, left = part[:half], part[half:]
    right = ring.send(right, 1)
    left = ring.send(left, -1)
    strip = gram_part(mine, other, "cols")
    step = 1
    while step < ring.length:
        strip = strip + swap(strip, "rows", step)
        step *= 2
    if columns % 4 == 0:
        strip = join((lax.axis_index("cols") >> 1) & 1, strip, swap(strip, "cols", 2))
    gram = gram_upper("cols", strip, swap(strip, "cols", 1))
    aheads = [sign * d for d in range(far - 1, 0, -1) for sign in (1, -1)] + [0]
    parts = products(ring, "cols", aheads[:2], False, stop, srest, top, rest)
    parts += products(ring, "cols", aheads[2:], False, stop, srest, top, rest)
    parts = dict(zip(aheads, parts))
    for d in range(far - 1, 0, -1):
        if d == far - 1:
            right = jnp.pad(right, ((0, half), (0, 0)))
            left = jnp.pad(left, ((half, 0), (0, 0)))
        right = ring.send(parts[d] + right, 1)
        left = ring.send(parts[-d] + left, -1)
    own = parts[0] + (right + left)
    panels = []
    while len(panels) * PANEL < gram.shape[0]:
        panels.append(factor_rows(gram, panels))
    early, late = {(0, 0): own}, {}
    right = left = own
    for d in range(1, far + 1):
        if d == far:
            right, left = right[:half], left[half:]
        right = ring.send(right, 1)
        left = ring.send(left, -1)
        held = early if d < far else late
        held[-d, 0] = right
        held[d, half if d == far else 0] = left
    out = final(ring, early, panels, size)
    projected = final(ring, late, panels, size, out)
    total = snapshot.shape[0] * lax.axis_size("rows")
    return (projected, upper_part(panels) / jnp.sqrt(jnp.float32(total)))


def plain_body(snapshot, test_matrix):
    sketch = lax.psum(mm(snapshot, test_matrix, ((1,), (0,))), "cols")
    gram = lax.psum(mm(sketch, sketch, ((0,), (0,))), "rows")
    panels = []
    while len(panels) * PANEL < gram.shape[0]:
        panels.append(factor_rows(gram, panels))
    product = lax.psum(mm(snapshot, sketch, ((0,), (0,))), "rows")
    total = snapshot.shape[0] * lax.axis_size("rows")
    projected = mm(product, lower_part(panels), ((1,), (1,)))
    return (projected, upper_part(panels) / jnp.sqrt(jnp.float32(total)))


def solution(mesh):
    return jax.shard_map(
        body,
        mesh=mesh,
        in_specs=(P("rows", "cols"), P("cols", None)),
        out_specs=(P("cols", None), P()),
        check_vma=False,
    )
```
